512 devices in a mesh: tok: 64 (over x, z, core), head: 8 (over y).
Axes of the slice: x: 4, y: 8, z: 8, core: 2. Of those that a mesh axis runs over, the one named last changes fastest.
Arguments:
- qkv: bfloat16 [3, 16384, 3072], P(None, 'tok', 'head'), may hold values from -8 to 8
- token_rank: int32 [48, 16384], P('head', 'tok'), may hold values from 0 to 16383, as said below
- cluster_sizes: int32 [48, 256], P('head'), may hold values from 1 to 381, as said below
- cluster_owner: int32 [48, 256], P('head'), may hold values from 0 to 63, as said below
- cache_zero: bfloat16 [16384, 3072], P('tok', 'head'), may hold values from -1.796875 to 1.796875
- cache_one: bfloat16 [16384, 3072], P('tok', 'head'), may hold values from -1.796875 to 1.796875
- cache_two: bfloat16 [16384, 3072], P('tok', 'head'), may hold values from -1.796875 to 1.796875
- cache_uncond: bfloat16 [16384, 3072], P('tok', 'head'), may hold values from -4 to 4
- norm_gain: float32 [3072], replicated, may hold values from 0.5 to 1.5
- norm_bias: float32 [3072], replicated, may hold values from -3 to 3
Outputs:
- normed: bfloat16 [16384, 3072], P(('tok', 'head'))
- taylor_zero: bfloat16 [16384, 3072], P('tok', 'head')
- taylor_one: bfloat16 [16384, 3072], P('tok', 'head')
- taylor_two: bfloat16 [16384, 3072], P('tok', 'head')
- taylor_three: bfloat16 [16384, 3072], P('tok', 'head')
The draws below stay inside these ranges and needn't reach their ends.
Inputs may be any that keep to these rules, and one draw needn't show every extreme that they name: `token_rank`: for each head a permutation of the tokens: the position of each token when the tokens are ordered by cluster, clusters in increasing number. `cluster_sizes`: for each head the sizes sum to 16384; every head has a cluster of exactly 381 tokens. `cluster_owner`: each group holds 4 clusters of every head and at most 384 tokens of a head, a bound that some group of every head reaches; of the tokens that one index of tok holds, at most 8 of one head lie in one group, a bound reached in every draw; heads 2j and 2j + 1 together have exactly 8 of those tokens in each group.
All inputs are finite; a program needn't handle non-finite values.
Results may differ from the reference program's by a relative error of at most 0.0059.
Values may be sent and summed in bfloat16 or wider, within the bound.
No kernel may reach another device: no remote copies, remote signals or barrier semaphores. Data moves between devices by JAX's collectives and lax.ppermute only.
A program may use at most 64 MiB of HBM per device.

```python
import math
import jax
import jax.numpy as jnp
from jax import lax

HEAD_DIM = 64
HEADS = 48
WIDTH = 3072
TOK_DEV = 256
TOKENS = 16384
CLD = 4
NCLUST = 256
CAP = 384
STEP_GAP = 2
N_TOK = 64


def layout_head(operands):
    head_key, pair_key, mirror = operands
    subkeys = jax.random.split(head_key, 7)
    pair_subkeys = jax.random.split(pair_key, 3)
    sign = 1 - 2 * mirror
    pair_mean = TOK_DEV // N_TOK
    shuffle = jax.random.permutation(pair_subkeys[0], N_TOK)
    shifts = jax.random.randint(pair_subkeys[1], (N_TOK // 2,), 0, pair_mean - 1)
    shifts = shifts.at[0].set(pair_mean - 2)
    per_source = jnp.zeros((N_TOK,), jnp.int32)
    per_source = per_source.at[shuffle[0::2]].set(pair_mean + sign * shifts)
    per_source = per_source.at[shuffle[1::2]].set(pair_mean - sign * shifts)
    pattern = jax.random.permutation(pair_subkeys[2], N_TOK)
    offsets = (sign * jnp.where(pattern < N_TOK // 2, 2, -2)).astype(jnp.int32)
    sources = jnp.arange(N_TOK, dtype=jnp.int32)
    counts = per_source[None, :] + offsets[(sources[:, None] - sources[None, :]) % N_TOK]
    count_ends = jnp.cumsum(counts, axis=1)
    local_keys = jax.random.split(subkeys[3], N_TOK)
    local_place = jax.vmap(lambda one_key: jax.random.permutation(one_key, TOK_DEV))(local_keys)
    targets = jnp.sum((count_ends[:, None, :] <= local_place[:, :, None]).astype(jnp.int32), axis=2).reshape(TOKENS)
    tie_break = jax.random.permutation(subkeys[4], TOKENS)
    ordering = jnp.argsort(targets * TOKENS + tie_break, stable=True)
    global_place = jnp.zeros((TOKENS,), jnp.int32).at[ordering].set(jnp.arange(TOKENS, dtype=jnp.int32))
    group_loads = N_TOK * per_source
    load_starts = jnp.cumsum(group_loads) - group_loads
    in_group = global_place - load_starts[targets]
    cut_points = jnp.sort(jax.random.randint(subkeys[5], (N_TOK, CLD - 1), 0, (group_loads - CLD + 1)[:, None]), axis=1)
    big_group = jnp.where(mirror == 1, shuffle[1], shuffle[0])
    cut_points = cut_points.at[big_group].set(0)
    cut_edges = jnp.concatenate([jnp.zeros((N_TOK, 1), jnp.int32), cut_points, (group_loads - CLD)[:, None]], axis=1)
    split_sizes = 1 + cut_edges[:, 1:] - cut_edges[:, :-1]
    cluster_ids = jnp.sort(jax.random.permutation(subkeys[6], NCLUST).reshape(N_TOK, CLD), axis=1)
    owner_row = jnp.zeros((NCLUST,), jnp.int32).at[cluster_ids.reshape(-1)].set(jnp.repeat(jnp.arange(N_TOK, dtype=jnp.int32), CLD))
    size_row = jnp.zeros((NCLUST,), jnp.int32).at[cluster_ids.reshape(-1)].set(split_sizes.reshape(-1))
    rank_starts = jnp.cumsum(size_row) - size_row
    split_ends = jnp.cumsum(split_sizes, axis=1)
    token_ends = split_ends[targets]
    within = jnp.sum((token_ends <= in_group[:, None]).astype(jnp.int32), axis=1)
    split_starts = split_ends - split_sizes
    offset_in = in_group - split_starts[targets, within]
    cluster_of = cluster_ids[targets, within]
    rank_row = rank_starts[cluster_of] + offset_in
    return (rank_row.astype(jnp.int32), size_row.astype(jnp.int32), owner_row.astype(jnp.int32))


def shared_layout(base_key):
    head_keys = jax.random.split(jax.random.fold_in(base_key, 17), HEADS)
    pair_keys = jnp.repeat(jax.random.split(jax.random.fold_in(base_key, 23), HEADS // 2), 2, axis=0)
    mirror = (jnp.arange(HEADS, dtype=jnp.int32) % 2).astype(jnp.int32)
    return lax.map(layout_head, (head_keys, pair_keys, mirror))


def draw_token_rank(key, part):
    return shared_layout(key)[0]


def draw_cluster_sizes(key, part):
    return shared_layout(key)[1]


def draw_cluster_owner(key, part):
    return shared_layout(key)[2]


def draw_qkv(key, part):
    subkeys = jax.random.split(jax.random.fold_in(key, 29), 1)
    base = jnp.clip(jax.random.normal(subkeys[0], (3, TOKENS, WIDTH), jnp.float32), -4.0, 4.0)
    scaled = base * jnp.array([1.0, 1.0, 2.0], jnp.float32)[:, None, None]
    return scaled.astype(jnp.bfloat16)


def draw_cache_uncond(key, part):
    subkeys = jax.random.split(jax.random.fold_in(key, 41), 3)
    row_scale = jnp.exp(jax.random.uniform(subkeys[1], (TOKENS, 1), jnp.float32, -2.302585, 0.0))
    column_scale = jnp.exp(jax.random.uniform(subkeys[2], (1, WIDTH), jnp.float32, -2.302585, 0.0))
    base = jnp.clip(jax.random.normal(subkeys[0], (TOKENS, WIDTH), jnp.float32), -4.0, 4.0)
    return (base * row_scale * column_scale).astype(jnp.bfloat16)


def levels(key, shape, cuts, smallest, high):
    def one(axis_at, shards_of):
        steps = jax.random.uniform(jax.random.fold_in(jax.random.fold_in(key, 6), axis_at), (shards_of,), jnp.float32, smallest / len(cuts), high / len(cuts))
        return jnp.repeat(jnp.exp(steps), shape[axis_at] // shards_of).reshape((-1,) + (1,) * (len(shape) - axis_at - 1))

    factor_of = one(*cuts[0])
    for cut in cuts[1:]:
        factor_of = factor_of * one(*cut)
    return factor_of


def bell_draw(own_key, dims, deviation, limit, cuts=(), kind=jnp.bfloat16):
    drawn = deviation * jax.random.normal(own_key, dims, jnp.float32)
    if cuts:
        drawn = drawn * levels(own_key, dims, cuts, -0.22, 0.18)
    return jnp.clip(drawn, -limit, limit).astype(kind)


def setup_inputs(seed: int = 0) -> dict:
    splits = jax.random.split(jax.random.key(seed), 11)
    qkv = draw_qkv(jax.random.fold_in(splits[10], 71), 0)
    token_rank = draw_token_rank(jax.random.fold_in(splits[10], 71), 0)
    cluster_sizes = draw_cluster_sizes(jax.random.fold_in(splits[10], 71), 0)
    cluster_owner = draw_cluster_owner(jax.random.fold_in(splits[10], 71), 0)
    cache_zero = bell_draw(splits[4], (TOKENS, WIDTH), 0.3, 1.796875, ((0, 64), (1, 8)))
    cache_one = bell_draw(splits[5], (TOKENS, WIDTH), 0.3, 1.796875, ((0, 64), (1, 8)))
    cache_two = bell_draw(splits[6], (TOKENS, WIDTH), 0.3, 1.796875, ((0, 64), (1, 8)))
    cache_uncond = draw_cache_uncond(jax.random.fold_in(splits[10], 71), 0)
    norm_gain = jnp.clip(1.0 + 0.1 * jax.random.normal(splits[8], (WIDTH,), jnp.float32), 0.5, 1.5)
    norm_bias = bell_draw(splits[9], (WIDTH,), 0.5, 3.0, (), jnp.float32)
    return dict(qkv=qkv, token_rank=token_rank, cluster_sizes=cluster_sizes, cluster_owner=cluster_owner, cache_zero=cache_zero, cache_one=cache_one, cache_two=cache_two, cache_uncond=cache_uncond, norm_gain=norm_gain, norm_bias=norm_bias)


guide_scale = 6.0
norm_eps = 1e-05

def group_attention(operands):
    queries, keys_in, values_in, groups, members = operands
    tokens_total = queries.shape[0]
    ordering = jnp.argsort(groups, stable=True).astype(jnp.int32)
    group_sizes = lax.optimization_barrier(jnp.sum((groups[:, None] == jnp.arange(N_TOK, dtype=jnp.int32)[None, :]).astype(jnp.int32), axis=0)).astype(jnp.int32)
    group_starts = (jnp.cumsum(group_sizes) - group_sizes).astype(jnp.int32)
    pad_rows = jnp.zeros((CAP, HEAD_DIM), queries.dtype)
    sorted_q = jnp.concatenate([queries[ordering], pad_rows], axis=0)
    sorted_k = jnp.concatenate([keys_in[ordering], pad_rows], axis=0)
    sorted_v = jnp.concatenate([values_in[ordering], pad_rows], axis=0)
    sorted_members = jnp.concatenate([members[ordering], jnp.full((CAP,), -1, jnp.int32)], axis=0)
    window = jnp.arange(CAP, dtype=jnp.int32)

    def one_group(carry, group_id):
        begin = group_starts[group_id]
        block_q = lax.dynamic_slice_in_dim(sorted_q, begin, CAP, 0)
        block_k = lax.dynamic_slice_in_dim(sorted_k, begin, CAP, 0)
        block_v = lax.dynamic_slice_in_dim(sorted_v, begin, CAP, 0)
        block_members = lax.dynamic_slice_in_dim(sorted_members, begin, CAP, 0)
        scores = lax.dot_general(block_q, block_k, (((1,), (1,)), ((), ())), preferred_element_type=jnp.float32) * (1.0 / math.sqrt(HEAD_DIM))
        allowed = block_members[:, None] == block_members[None, :]
        masked = jnp.where(allowed, scores, -jnp.inf)
        largest = lax.optimization_barrier(jnp.max(masked, axis=1, keepdims=True))
        expo = jnp.where(allowed, jnp.exp(masked - largest), 0.0)
        totals = lax.optimization_barrier(jnp.sum(expo, axis=1, keepdims=True))
        probability = (expo / totals).astype(jnp.bfloat16)
        result = jnp.dot(probability, block_v, preferred_element_type=jnp.float32).astype(jnp.bfloat16)
        result = lax.optimization_barrier(result).astype(jnp.float32)
        valid = window < group_sizes[group_id]
        carry = carry.at[begin + window].add(jnp.where(valid[:, None], result, 0.0))
        return (carry, None)
    start_total = jnp.zeros((tokens_total + CAP, HEAD_DIM), jnp.float32)
    summed = lax.scan(one_group, start_total, jnp.arange(N_TOK, dtype=jnp.int32))[0]
    in_order = summed[:tokens_total]
    return jnp.zeros((tokens_total, HEAD_DIM), jnp.float32).at[ordering].set(in_order)

def head_groups(operands):
    rank_row, ends_row, owner_row = operands
    members = lax.optimization_barrier(jnp.sum((ends_row[None, :] <= rank_row[:, None]).astype(jnp.int32), axis=1)).astype(jnp.int32)
    return (members, owner_row[members])

def reference(qkv, token_rank, cluster_sizes, cluster_owner, cache_zero, cache_one, cache_two, cache_uncond, norm_gain, norm_bias):
    cluster_ends = jnp.cumsum(cluster_sizes, axis=1).astype(jnp.int32)
    members, groups = lax.map(head_groups, (token_rank, cluster_ends, cluster_owner))
    per_head = qkv.reshape(3, TOKENS, HEADS, HEAD_DIM).transpose(0, 2, 1, 3)
    outputs = lax.map(group_attention, (per_head[0], per_head[1], per_head[2], groups, members))
    taylor_zero = outputs.transpose(1, 0, 2).reshape(TOKENS, WIDTH).astype(jnp.bfloat16)
    attention_wide = taylor_zero.astype(jnp.float32)
    first_diff = (attention_wide - cache_zero.astype(jnp.float32)) / STEP_GAP
    second_diff = (first_diff - cache_one.astype(jnp.float32)) / STEP_GAP
    third_diff = (second_diff - cache_two.astype(jnp.float32)) / STEP_GAP
    uncond_wide = cache_uncond.astype(jnp.float32)
    guided = (uncond_wide + guide_scale * (attention_wide - uncond_wide)).astype(jnp.bfloat16)
    widened = lax.optimization_barrier(guided).astype(jnp.float32)
    row_mean = lax.optimization_barrier(jnp.mean(widened, axis=1, keepdims=True))
    centered = widened - row_mean
    row_var = lax.optimization_barrier(jnp.mean(centered * centered, axis=1, keepdims=True))
    normed = (centered * lax.rsqrt(row_var + norm_eps) * norm_gain + norm_bias).astype(jnp.bfloat16)
    return (normed, taylor_zero, first_diff.astype(jnp.bfloat16), second_diff.astype(jnp.bfloat16), third_diff.astype(jnp.bfloat16))
```

```python
import jax
import jax.numpy as jnp
from jax import lax
from jax.experimental import pallas as pl
from jax.experimental.pallas import tpu as pltpu
from jax.sharding import Mesh
from jax.sharding import PartitionSpec as P

HEAD_DIM = 64
TOK = ("tok_0", "tok_1", "tok_2")
TOK_HEAD = ("tok_0", "tok_1", "tok_2", "head")
GROUPS = 64
PAIR_ROWS = 8
MASK_OUT = 32768.0
GUIDE_SCALE = 6.0
NORM_EPS = 1e-05
F32, BF16, I32 = jnp.float32, jnp.bfloat16, jnp.int32
NT = (((1,), (1,)), ((), ()))


def iota(shape, dim):
    return lax.broadcasted_iota(I32, shape, dim)


def ones_where(cond):
    return jnp.where(cond, 1.0, 0.0).astype(BF16)


def matmul(a, b):
    return jnp.dot(a, b, preferred_element_type=F32)


def swap_halves(x):
    return pltpu.roll(x, HEAD_DIM, 1)


def pack_kernel(qkv_ref, rank_ref, sizes_ref, owner_ref, send_ref, slot_ref):
    heads, tokens = rank_ref.shape
    clusters = sizes_ref.shape[1]
    pairs = heads // 2
    slots = GROUPS * PAIR_ROWS
    before = ones_where(iota((tokens, tokens), 0) < iota((tokens, tokens), 1))
    upto = ones_where(iota((clusters, clusters), 1) <= iota((clusters, clusters), 0))
    sizes = sizes_ref[...]
    low = (sizes & 255).astype(F32).astype(BF16)
    high = (sizes >> 8).astype(F32).astype(BF16)
    strict = ones_where(iota((clusters, clusters), 1) < iota((clusters, clusters), 0))

    def running(tri):
        return lax.dot_general(tri, low, NT, preferred_element_type=F32) + 256.0 * lax.dot_general(
            tri, high, NT, preferred_element_type=F32
        )

    ends, starts = running(upto), running(strict)
    group_id = iota((GROUPS, 1), 0).astype(F32) * float(PAIR_ROWS)
    left = iota((tokens, 2 * HEAD_DIM), 1) < HEAD_DIM
    values_01 = None
    values_2 = None
    slot_rows = []
    for j in range(pairs):
        places, labels = [], []
        offset = jnp.zeros((GROUPS, 1), F32)
        for half in range(2):
            h = 2 * j + half
            rank = rank_ref[h : h + 1, :].astype(F32)
            member = ones_where((starts[:, h : h + 1] <= rank) & (rank < ends[:, h : h + 1]))
            owned = ones_where(iota((GROUPS, clusters), 0) == owner_ref[h : h + 1, :])
            nth = jnp.sum(owned.astype(F32) * matmul(owned, before), axis=0, keepdims=True)
            label = jnp.where(iota((8, clusters), 0) - 4 * half == nth.astype(I32), 1.0, 0.0)
            rows = matmul(jnp.concatenate([owned.astype(F32), label], axis=0).astype(BF16), member)
            dest = rows[:GROUPS]
            labels.append(rows[GROUPS:])
            earlier = matmul(dest.astype(BF16), before)
            slot = jnp.sum(dest * (group_id + earlier + offset), axis=0, keepdims=True)
            offset = offset + jnp.sum(dest, axis=1, keepdims=True)
            slot_rows.append(slot)
            places.append(ones_where(iota((slots, tokens), 0) == slot.astype(I32)))
        cols = slice(2 * HEAD_DIM * j, 2 * HEAD_DIM * (j + 1))
        q, k, v = (qkv_ref[i, :, cols].astype(F32) for i in range(3))
        qs, ks, vs = swap_halves(q), swap_halves(k), swap_halves(v)
        if j == 1:
            v_even, v_odd = jnp.where(left, 0.0, vs), jnp.where(left, 0.0, v)
        else:
            v_even, v_odd = jnp.where(left, v, 0.0), jnp.where(left, vs, 0.0)
        rhs = jnp.concatenate(
            [
                jnp.concatenate([jnp.where(left, q, ks), v_even], axis=1),
                jnp.concatenate([jnp.where(left, qs, k), v_odd], axis=1),
            ],
            axis=0,
        ).astype(BF16)
        place = jnp.concatenate(places, axis=1)
        sorted_rows = matmul(place, rhs)
        label_rows = jnp.concatenate(labels, axis=1)
        parts = [jnp.zeros((HEAD_DIM + 8 * j, 2 * tokens), F32), label_rows]
        parts.append(jnp.zeros((HEAD_DIM - 8 * (j + 1), 2 * tokens), F32))
        label_lanes = lax.dot_general(
            place, jnp.concatenate(parts, axis=0).astype(BF16), NT, preferred_element_type=F32
        )
        send_ref[:, 8 * j : 8 * (j + 1), :] = (
            sorted_rows[:, : 2 * HEAD_DIM].reshape(GROUPS, 8, 2 * HEAD_DIM).astype(BF16)
        )
        v_rows = sorted_rows[:, 2 * HEAD_DIM :]
        if j == 0:
            values_01, values_2 = v_rows, label_lanes
        elif j == 1:
            values_01, values_2 = values_01 + v_rows, values_2 + label_lanes
        else:
            values_2 = values_2 + v_rows + label_lanes
    send_ref[:, 24:32, :] = values_01.reshape(GROUPS, 8, 2 * HEAD_DIM).astype(BF16)
    send_ref[:, 32:40, :] = values_2.reshape(GROUPS, 8, 2 * HEAD_DIM).astype(BF16)
    slot_rows.append(jnp.zeros((8 - heads, tokens), F32))
    slot_ref[...] = jnp.concatenate(slot_rows, axis=0)


def attend_kernel(recv_ref, back_ref):
    rows = GROUPS * PAIR_ROWS
    wide = 2 * HEAD_DIM

    def block(k):
        return recv_ref[:, 8 * k : 8 * (k + 1), :].reshape(rows, wide)

    lane = iota((rows, wide), 1)
    left = lane < HEAD_DIM
    values_01, values_2 = block(3), block(4)
    marks = values_2.astype(F32)
    outs = []
    for j in range(3):
        qk = block(j).astype(F32)
        own = (lane >= HEAD_DIM + 8 * j) & (lane < HEAD_DIM + 8 * (j + 1))
        a = jnp.where(left, qk, marks).astype(BF16)
        b = jnp.where(
            left, swap_halves(qk), jnp.where(own, MASK_OUT * (marks - 1.0), 0.0)
        ).astype(BF16)
        scores = lax.dot_general(a, b, NT, preferred_element_type=F32)
        largest = jnp.max(scores, axis=1, keepdims=True)
        expo = jnp.exp((scores - largest) * 0.125)
        totals = jnp.sum(expo, axis=1, keepdims=True)
        probs = (expo * (1.0 / totals)).astype(BF16)
        outs.append(matmul(probs, values_2 if j == 2 else values_01))
    back_ref[:, 0:8, :] = jnp.where(left, outs[0], outs[1]).reshape(GROUPS, 8, wide).astype(BF16)
    back_ref[:, 8:16, :] = outs[2].reshape(GROUPS, 8, wide).astype(BF16)


def finish_kernel(
    back_ref, slot_ref, c0_ref, c1_ref, c2_ref, un_ref, zero_ref, one_ref, two_ref, three_ref, guided_ref
):
    tokens = slot_ref.shape[1]
    rows = GROUPS * PAIR_ROWS
    wide = 2 * HEAD_DIM
    slot = jnp.transpose(slot_ref[...]).astype(I32)
    pos = iota((tokens, rows), 1)
    o01 = back_ref[:, 0:8, :].reshape(rows, wide)
    o2 = back_ref[:, 8:16, :].reshape(rows, wide)
    o10 = swap_halves(o01.astype(F32)).astype(BF16)
    o2s = swap_halves(o2.astype(F32)).astype(BF16)
    left = iota((tokens, wide), 1) < HEAD_DIM
    for j, (even, odd) in enumerate(((o01, o10), (o10, o01), (o2, o2s))):
        low = matmul(ones_where(slot[:, 2 * j : 2 * j + 1] == pos), even)
        high = matmul(ones_where(slot[:, 2 * j + 1 : 2 * j + 2] == pos), odd)
        att = jnp.where(left, low, high)
        cols = slice(wide * j, wide * (j + 1))
        zero_ref[:, cols] = att.astype(BF16)
        first = (att - c0_ref[:, cols].astype(F32)) * 0.5
        second = (first - c1_ref[:, cols].astype(F32)) * 0.5
        third = (second - c2_ref[:, cols].astype(F32)) * 0.5
        one_ref[:, cols] = first.astype(BF16)
        two_ref[:, cols] = second.astype(BF16)
        three_ref[:, cols] = third.astype(BF16)
        un = un_ref[:, cols].astype(F32)
        guided_ref[:, cols] = (un + GUIDE_SCALE * (att - un)).astype(BF16)


def norm_kernel(rows_ref, gain_ref, bias_ref, out_ref):
    parts, _, width = rows_ref.shape
    total = parts * width
    blocks = [rows_ref[i].astype(F32) for i in range(parts)]
    mean = sum(jnp.sum(b, axis=1, keepdims=True) for b in blocks) * (1.0 / total)
    blocks = [b - mean for b in blocks]
    var = sum(jnp.sum(b * b, axis=1, keepdims=True) for b in blocks) * (1.0 / total)
    scale = lax.rsqrt(var + NORM_EPS)
    for i, b in enumerate(blocks):
        cols = slice(width * i, width * (i + 1))
        out_ref[:, cols] = (b * scale * gain_ref[:, cols] + bias_ref[:, cols]).astype(BF16)


def call(kernel, outs, *args, **kw):
    vmem = pl.BlockSpec(memory_space=pltpu.VMEM)
    return pl.pallas_call(
        kernel,
        out_shape=[jax.ShapeDtypeStruct(s, t) for s, t in outs],
        in_specs=[vmem] * len(args),
        out_specs=[vmem] * len(outs),
        **kw,
    )(*args)


def pack(qkv, token_rank, cluster_sizes, cluster_owner, **kw):
    tokens = token_rank.shape[1]
    outs = [((GROUPS, 40, 128), BF16), ((8, tokens), F32)]
    return call(pack_kernel, outs, qkv, token_rank, cluster_sizes, cluster_owner, **kw)


def attend(arrived, **kw):
    return call(attend_kernel, [((GROUPS, 16, 128), BF16)], arrived, **kw)[0]


def finish(back, slots, c0, c1, c2, un, **kw):
    return call(finish_kernel, [(c0.shape, BF16)] * 5, back, slots, c0, c1, c2, un, **kw)


def norm(rows, gain, bias, **kw):
    parts, count, width = rows.shape
    outs = [((count, parts * width), BF16)]
    return call(norm_kernel, outs, rows, gain.reshape(1, -1), bias.reshape(1, -1), **kw)[0]


def on_device(qkv, rank, sizes, owner, c0, c1, c2, un, gain, bias):
    send, slots = pack(qkv, rank, sizes, owner)
    arrived = lax.all_to_all(send, TOK, split_axis=0, concat_axis=0, tiled=True)
    back = lax.all_to_all(attend(arrived), TOK, split_axis=0, concat_axis=0, tiled=True)
    zero, one, two, three, guided = finish(back, slots, c0, c1, c2, un)
    blocks = guided.reshape(8, guided.shape[0] // 8, guided.shape[1])
    rows = lax.all_to_all(blocks, "head", split_axis=0, concat_axis=0, tiled=True)
    return norm(rows, gain, bias), zero, one, two, three


def solution(mesh):
    torus = Mesh(mesh.devices.reshape(4, 8, 2, mesh.shape["head"]), TOK_HEAD)
    in_specs = (
        P(None, TOK, "head"),
        P("head", TOK),
        P("head", None),
        P("head", None),
        P(TOK, "head"),
        P(TOK, "head"),
        P(TOK, "head"),
        P(TOK, "head"),
        P(),
        P(),
    )
    out_specs = (P(TOK_HEAD, None), P(TOK, "head"), P(TOK, "head"), P(TOK, "head"), P(TOK, "head"))
    return jax.shard_map(
        on_device, mesh=torus, in_specs=in_specs, out_specs=out_specs, check_vma=False
    )
```

```python
import jax
import jax.numpy as jnp
from jax import lax
from jax.experimental import pallas as pl
from jax.experimental.pallas import tpu as pltpu
from jax.sharding import Mesh
from jax.sharding import PartitionSpec as P

HEAD_DIM = 64
TOK = ("tok_0", "tok_1", "tok_2")
TOK_HEAD = ("tok_0", "tok_1", "tok_2", "head")
GROUPS = 64
PAIR_ROWS = 8
MASK_OUT = 32768.0
GUIDE_SCALE = 6.0
NORM_EPS = 1e-05
F32, BF16, I32 = jnp.float32, jnp.bfloat16, jnp.int32
NT = (((1,), (1,)), ((), ()))


def iota(shape, dim):
    return lax.broadcasted_iota(I32, shape, dim)


def ones_where(cond):
    return jnp.where(cond, 1.0, 0.0).astype(BF16)


def matmul(a, b):
    return jnp.dot(a, b, preferred_element_type=F32)


def swap_halves(x):
    return pltpu.roll(x, HEAD_DIM, 1)


def pack_kernel(qkv_ref, rank_ref, sizes_ref, owner_ref, send_ref, slot_ref):
    heads, tokens = rank_ref.shape
    clusters = sizes_ref.shape[1]
    pairs = heads // 2
    slots = GROUPS * PAIR_ROWS
    before = ones_where(iota((tokens, tokens), 0) < iota((tokens, tokens), 1))
    upto = ones_where(iota((clusters, clusters), 1) <= iota((clusters, clusters), 0))
    sizes = sizes_ref[...]
    low = (sizes & 255).astype(F32).astype(BF16)
    high = (sizes >> 8).astype(F32).astype(BF16)
    strict = ones_where(iota((clusters, clusters), 1) < iota((clusters, clusters), 0))

    def running(tri):
        return lax.dot_general(tri, low, NT, preferred_element_type=F32) + 256.0 * lax.dot_general(
            tri, high, NT, preferred_element_type=F32
        )

    ends, starts = running(upto), running(strict)
    group_id = iota((GROUPS, 1), 0).astype(F32) * float(PAIR_ROWS)
    left = iota((tokens, 2 * HEAD_DIM), 1) < HEAD_DIM
    values_01 = None
    values_2 = None
    slot_rows = []
    for j in range(pairs):
        places, labels = [], []
        offset = jnp.zeros((GROUPS, 1), F32)
        for half in range(2):
            h = 2 * j + half
            rank = rank_ref[h : h + 1, :].astype(F32)
            member = ones_where((starts[:, h : h + 1] <= rank) & (rank < ends[:, h : h + 1]))
            owned = ones_where(iota((GROUPS, clusters), 0) == owner_ref[h : h + 1, :])
            nth = jnp.sum(owned.astype(F32) * matmul(owned, before), axis=0, keepdims=True)
            label = jnp.where(iota((8, clusters), 0) - 4 * half == nth.astype(I32), 1.0, 0.0)
            rows = matmul(jnp.concatenate([owned.astype(F32), label], axis=0).astype(BF16), member)
            dest = rows[:GROUPS]
            labels.append(rows[GROUPS:])
            earlier = matmul(dest.astype(BF16), before)
            slot = jnp.sum(dest * (group_id + earlier + offset), axis=0, keepdims=True)
            offset = offset + jnp.sum(dest, axis=1, keepdims=True)
            slot_rows.append(slot)
            places.append(ones_where(iota((slots, tokens), 0) == slot.astype(I32)))
        cols = slice(2 * HEAD_DIM * j, 2 * HEAD_DIM * (j + 1))
        q, k, v = (qkv_ref[i, :, cols].astype(F32) for i in range(3))
        qs, ks, vs = swap_halves(q), swap_halves(k), swap_halves(v)
        if j == 1:
            v_even, v_odd = jnp.where(left, 0.0, vs), jnp.where(left, 0.0, v)
        else:
            v_even, v_odd = jnp.where(left, v, 0.0), jnp.where(left, vs, 0.0)
        rhs = jnp.concatenate(
            [
                jnp.concatenate([jnp.where(left, q, ks), v_even], axis=1),
                jnp.concatenate([jnp.where(left, qs, k), v_odd], axis=1),
            ],
            axis=0,
        ).astype(BF16)
        place = jnp.concatenate(places, axis=1)
        sorted_rows = matmul(place, rhs)
        label_rows = jnp.concatenate(labels, axis=1)
        parts = [jnp.zeros((HEAD_DIM + 8 * j, 2 * tokens), F32), label_rows]
        parts.append(jnp.zeros((HEAD_DIM - 8 * (j + 1), 2 * tokens), F32))
        label_lanes = lax.dot_general(
            place, jnp.concatenate(parts, axis=0).astype(BF16), NT, preferred_element_type=F32
        )
        send_ref[:, 8 * j : 8 * (j + 1), :] = (
            sorted_rows[:, : 2 * HEAD_DIM].reshape(GROUPS, 8, 2 * HEAD_DIM).astype(BF16)
        )
        v_rows = sorted_rows[:, 2 * HEAD_DIM :]
        if j == 0:
            values_01, values_2 = v_rows, label_lanes
        elif j == 1:
            values_01, values_2 = values_01 + v_rows, values_2 + label_lanes
        else:
            values_2 = values_2 + v_rows + label_lanes
    send_ref[:, 24:32, :] = values_01.reshape(GROUPS, 8, 2 * HEAD_DIM).astype(BF16)
    send_ref[:, 32:40, :] = values_2.reshape(GROUPS, 8, 2 * HEAD_DIM).astype(BF16)
    slot_rows.append(jnp.zeros((8 - heads, tokens), F32))
    slot_ref[...] = jnp.concatenate(slot_rows, axis=0)


def attend_kernel(recv_ref, back_ref):
    rows = GROUPS * PAIR_ROWS
    wide = 2 * HEAD_DIM

    def block(k):
        return recv_ref[:, 8 * k : 8 * (k + 1), :].reshape(rows, wide)

    lane = iota((rows, wide), 1)
    left = lane < HEAD_DIM
    values_01, values_2 = block(3), block(4)
    marks = values_2.astype(F32)
    outs = []
    for j in range(3):
        qk = block(j).astype(F32)
        own = (lane >= HEAD_DIM + 8 * j) & (lane < HEAD_DIM + 8 * (j + 1))
        a = jnp.where(left, qk, marks).astype(BF16)
        b = jnp.where(
            left, swap_halves(qk), jnp.where(own, MASK_OUT * (marks - 1.0), 0.0)
        ).astype(BF16)
        scores = lax.dot_general(a, b, NT, preferred_element_type=F32)
        largest = jnp.max(scores, axis=1, keepdims=True)
        expo = jnp.exp((scores - largest) * 0.125)
        totals = jnp.sum(expo, axis=1, keepdims=True)
        probs = (expo * (1.0 / totals)).astype(BF16)
        outs.append(matmul(probs, values_2 if j == 2 else values_01))
    back_ref[:, 0:8, :] = jnp.where(left, outs[0], outs[1]).reshape(GROUPS, 8, wide).astype(BF16)
    back_ref[:, 8:16, :] = outs[2].reshape(GROUPS, 8, wide).astype(BF16)


def finish_kernel(
    back_ref, slot_ref, c0_ref, c1_ref, c2_ref, un_ref, zero_ref, one_ref, two_ref, three_ref, guided_ref
):
    tokens = slot_ref.shape[1]
    rows = GROUPS * PAIR_ROWS
    wide = 2 * HEAD_DIM
    slot = jnp.transpose(slot_ref[...]).astype(I32)
    pos = iota((tokens, rows), 1)
    o01 = back_ref[:, 0:8, :].reshape(rows, wide)
    o2 = back_ref[:, 8:16, :].reshape(rows, wide)
    o10 = swap_halves(o01.astype(F32)).astype(BF16)
    o2s = swap_halves(o2.astype(F32)).astype(BF16)
    left = iota((tokens, wide), 1) < HEAD_DIM
    for j, (even, odd) in enumerate(((o01, o10), (o10, o01), (o2, o2s))):
        low = matmul(ones_where(slot[:, 2 * j : 2 * j + 1] == pos), even)
        high = matmul(ones_where(slot[:, 2 * j + 1 : 2 * j + 2] == pos), odd)
        att = jnp.where(left, low, high)
        cols = slice(wide * j, wide * (j + 1))
        zero_ref[:, cols] = att.astype(BF16)
        first = (att - c0_ref[:, cols].astype(F32)) * 0.5
        second = (first - c1_ref[:, cols].astype(F32)) * 0.5
        third = (second - c2_ref[:, cols].astype(F32)) * 0.5
        one_ref[:, cols] = first.astype(BF16)
        two_ref[:, cols] = second.astype(BF16)
        three_ref[:, cols] = third.astype(BF16)
        un = un_ref[:, cols].astype(F32)
        guided_ref[:, cols] = (un + GUIDE_SCALE * (att - un)).astype(BF16)


def norm_kernel(rows_ref, gain_ref, bias_ref, out_ref):
    parts, _, width = rows_ref.shape
    total = parts * width
    blocks = [rows_ref[i].astype(F32) for i in range(parts)]
    mean = sum(jnp.sum(b, axis=1, keepdims=True) for b in blocks) * (1.0 / total)
    blocks = [b - mean for b in blocks]
    var = sum(jnp.sum(b * b, axis=1, keepdims=True) for b in blocks) * (1.0 / total)
    scale = lax.rsqrt(var + NORM_EPS)
    for i, b in enumerate(blocks):
        cols = slice(width * i, width * (i + 1))
        out_ref[:, cols] = (b * scale * gain_ref[:, cols] + bias_ref[:, cols]).astype(BF16)


def call(kernel, outs, *args, **kw):
    vmem = pl.BlockSpec(memory_space=pltpu.VMEM)
    return pl.pallas_call(
        kernel,
        out_shape=[pltpu.VMEM(s, t) if stay else jax.ShapeDtypeStruct(s, t) for s, t, stay in outs],
        in_specs=[vmem] * len(args),
        out_specs=[vmem] * len(outs),
        **kw,
    )(*args)


def in_vmem(x):
    return pltpu.with_memory_space_constraint(x, pltpu.VMEM)


def pack(qkv, token_rank, cluster_sizes, cluster_owner, **kw):
    tokens = token_rank.shape[1]
    outs = [((GROUPS, 40, 128), BF16, True), ((8, tokens), F32, True)]
    return call(pack_kernel, outs, qkv, token_rank, cluster_sizes, cluster_owner, **kw)


def attend(arrived, **kw):
    return call(attend_kernel, [((GROUPS, 16, 128), BF16, True)], in_vmem(arrived), **kw)[0]


def finish(back, slots, c0, c1, c2, un, **kw):
    outs = [(c0.shape, BF16, True)] * 5
    ins = [in_vmem(x) for x in (back, slots, c0, c1, c2, un)]
    return call(finish_kernel, outs, *ins, **kw)


def norm(rows, gain, bias, **kw):
    parts, count, width = rows.shape
    outs = [((count, parts * width), BF16, False)]
    return call(norm_kernel, outs, in_vmem(rows), in_vmem(gain.reshape(1, -1)), in_vmem(bias.reshape(1, -1)), **kw)[0]


def on_device(qkv, rank, sizes, owner, c0, c1, c2, un, gain, bias):
    send, slots = pack(qkv, rank, sizes, owner)
    arrived = lax.all_to_all(send, TOK, split_axis=0, concat_axis=0, tiled=True)
    back = lax.all_to_all(attend(arrived), TOK, split_axis=0, concat_axis=0, tiled=True)
    zero, one, two, three, guided = finish(back, slots, c0, c1, c2, un)
    blocks = guided.reshape(8, guided.shape[0] // 8, guided.shape[1])
    rows = lax.all_to_all(blocks, "head", split_axis=0, concat_axis=0, tiled=True)
    return norm(rows, gain, bias), zero, one, two, three


def solution(mesh):
    torus = Mesh(mesh.devices.reshape(4, 8, 2, mesh.shape["head"]), TOK_HEAD)
    in_specs = (
        P(None, TOK, "head"),
        P("head", TOK),
        P("head", None),
        P("head", None),
        P(TOK, "head"),
        P(TOK, "head"),
        P(TOK, "head"),
        P(TOK, "head"),
        P(),
        P(),
    )
    out_specs = (P(TOK_HEAD, None), P(TOK, "head"), P(TOK, "head"), P(TOK, "head"), P(TOK, "head"))
    return jax.shard_map(
        on_device, mesh=torus, in_specs=in_specs, out_specs=out_specs, check_vma=False
    )
```

```python
import math

import jax
import jax.numpy as jnp
from jax import lax
from jax.experimental import pallas as pl
from jax.experimental.pallas import tpu as pltpu
from jax.sharding import Mesh
from jax.sharding import PartitionSpec as P

HEAD_DIM = 64
TOK = ("tok_0", "tok_1", "tok_2")
TOK_HEAD = ("tok_0", "tok_1", "tok_2", "head")
GROUPS = 64
PAIR_ROWS = 8
MASK_OUT = 32768.0
GUIDE_SCALE = 6.0
NORM_EPS = 1e-05
EXPONENT = math.log2(math.e) / math.sqrt(HEAD_DIM)
F32, BF16, I32 = jnp.float32, jnp.bfloat16, jnp.int32
NT = (((1,), (1,)), ((), ()))


def iota(shape, dim):
    return lax.broadcasted_iota(I32, shape, dim)


def ones_where(cond):
    return jnp.where(cond, 1.0, 0.0).astype(BF16)


def one_hot(cond):
    return jnp.where(cond, jnp.ones(cond.shape, BF16), jnp.zeros(cond.shape, BF16))


def matmul(a, b):
    return jnp.dot(a, b, preferred_element_type=F32)


def swap_halves(x):
    return pltpu.roll(x, HEAD_DIM, 1)


def pack_kernel(
    parity_ref, qkv_hbm, rank_ref, sizes_ref, owner_ref, send_ref, row_ref, qkv_ref, sem
):
    fetch = pltpu.make_async_copy(qkv_hbm, qkv_ref, sem)
    fetch.start()
    heads, tokens = rank_ref.shape
    clusters = sizes_ref.shape[1]
    pairs = heads // 2
    slots = GROUPS * PAIR_ROWS
    before = ones_where(iota((tokens, tokens), 0) < iota((tokens, tokens), 1))
    strict = ones_where(iota((clusters, clusters), 1) < iota((clusters, clusters), 0))
    sizes = sizes_ref[...]
    low = (sizes & 255).astype(F32).astype(BF16)
    high = (sizes >> 8).astype(F32).astype(BF16)
    starts = lax.dot_general(strict, low, NT, preferred_element_type=F32)
    starts = starts + 256.0 * lax.dot_general(strict, high, NT, preferred_element_type=F32)
    owned = [
        jnp.where(iota((GROUPS, clusters), 0) == owner_ref[h : h + 1, :], 1.0, 0.0)
        for h in range(heads)
    ]
    counts = matmul(jnp.concatenate(owned, axis=0).astype(BF16), before)
    first = iota((GROUPS + 8, clusters), 1) == 0
    dests, labels = [], []
    for h in range(heads):
        nth = jnp.sum(owned[h] * counts[GROUPS * h : GROUPS * (h + 1)], axis=0, keepdims=True)
        label = jnp.where(iota((8, clusters), 0) - 4 * (h % 2) == nth.astype(I32), 1.0, 0.0)
        table = jnp.concatenate([owned[h], label], axis=0)
        step = table - jnp.where(first, 0.0, pltpu.roll(table, 1, 1))
        reached = ones_where(starts[:, h : h + 1] <= rank_ref[h : h + 1, :].astype(F32))
        rows = matmul(step.astype(BF16), reached)
        dests.append(rows[:GROUPS])
        labels.append(rows[GROUPS:])
    earlier = matmul(jnp.concatenate(dests, axis=0).astype(BF16), before)
    group_id = iota((GROUPS, 1), 0).astype(F32) * float(PAIR_ROWS)
    slots_iota = iota((slots, tokens), 0).astype(jnp.int16)
    slot_rows, places = [], []
    for h in range(heads):
        offset = group_id
        if h % 2:
            offset = offset + jnp.sum(dests[h - 1], axis=1, keepdims=True)
        ahead = earlier[GROUPS * h : GROUPS * (h + 1)] + offset
        slot = jnp.sum(dests[h] * ahead, axis=0, keepdims=True)
        slot_rows.append(slot)
        places.append(one_hot(slots_iota == slot.astype(I32).astype(jnp.int16)))
    slot = jnp.concatenate(slot_rows, axis=0).astype(I32)
    group, place = slot >> 3, slot & 7
    mixed_row = 12 * group + 4 * parity_ref[0] + place
    last_row = 12 * group + 8 - 8 * parity_ref[0] + (place & 3)
    back_row = jnp.where(iota(slot.shape, 0) < 4, mixed_row, last_row)
    row_ref[...] = jnp.concatenate([back_row, place[4:6] >> 2], axis=0).astype(F32)
    left = iota((tokens, 2 * HEAD_DIM), 1) < HEAD_DIM
    lane = iota((tokens, 2 * HEAD_DIM), 1)
    marks = []
    for half in range(2):
        zeros = jnp.zeros((HEAD_DIM, tokens), F32)
        rest = jnp.zeros((HEAD_DIM - 8 * pairs, tokens), F32)
        marks.append(jnp.transpose(jnp.concatenate([zeros, *labels[half::2], rest], axis=0)))
    fetch.wait()
    values = []
    for j in range(pairs):
        cols = slice(2 * HEAD_DIM * j, 2 * HEAD_DIM * (j + 1))
        own = (lane >= HEAD_DIM + 8 * j) & (lane < HEAD_DIM + 8 * (j + 1))
        even, odd = (jnp.where(own, m, 0.0) for m in marks)
        q, k, v = (qkv_ref[i, :, cols].astype(F32) for i in range(3))
        qs, ks, vs = swap_halves(q), swap_halves(k), swap_halves(v)
        even = jnp.concatenate([jnp.where(left, q, ks), jnp.where(left, v, even)], axis=1)
        odd = jnp.concatenate([jnp.where(left, qs, k), jnp.where(left, vs, odd)], axis=1)
        place = jnp.concatenate(places[2 * j : 2 * j + 2], axis=1)
        sorted_rows = matmul(place, jnp.concatenate([even, odd], axis=0).astype(BF16))
        send_ref[:, 8 * j : 8 * (j + 1), :] = (
            sorted_rows[:, : 2 * HEAD_DIM].reshape(GROUPS, 8, 2 * HEAD_DIM).astype(BF16)
        )
        values.append(sorted_rows[:, 2 * HEAD_DIM :])
    left = iota((slots, 2 * HEAD_DIM), 1) < HEAD_DIM
    first = jnp.where(left, values[0], swap_halves(values[1]))
    second = jnp.where(left, values[2], values[0] + values[1] + values[2])
    send_ref[:, 24:32, :] = first.reshape(GROUPS, 8, 2 * HEAD_DIM).astype(BF16)
    send_ref[:, 32:40, :] = second.reshape(GROUPS, 8, 2 * HEAD_DIM).astype(BF16)


def attend_kernel(recv_ref, back_ref):
    rows = GROUPS * PAIR_ROWS
    wide = 2 * HEAD_DIM

    def block(k):
        return recv_ref[:, 8 * k : 8 * (k + 1), :].reshape(rows, wide)

    lane = iota((rows, wide), 1)
    left = lane < HEAD_DIM
    values_01 = block(3)
    marks = block(4).astype(F32)
    values_2 = jnp.where(left, marks, swap_halves(marks)).astype(BF16)
    outs = []
    for j in range(3):
        qk = block(j).astype(F32)
        own = (lane >= HEAD_DIM + 8 * j) & (lane < HEAD_DIM + 8 * (j + 1))
        a = jnp.where(left, qk, marks).astype(BF16)
        b = jnp.where(
            left, swap_halves(qk), jnp.where(own, MASK_OUT * (marks - 1.0), 0.0)
        ).astype(BF16)
        scores = lax.dot_general(a, b, NT, preferred_element_type=F32)
        largest = jnp.max(scores, axis=1, keepdims=True)
        expo = jnp.exp2((scores - largest) * EXPONENT)
        totals = jnp.sum(expo, axis=1, keepdims=True)
        probs = (expo * (1.0 / totals)).astype(BF16)
        outs.append(matmul(probs, values_2 if j == 2 else values_01))
    shape = (GROUPS // 2, 2, 8, wide)
    mixed = jnp.where(left, outs[0], outs[1]).reshape(shape).astype(BF16)
    back_ref[:, 0:8, :] = mixed[:, 0]
    back_ref[:, 16:24, :] = mixed[:, 1]
    last = outs[2].reshape(GROUPS, 8, wide)
    turned = pltpu.roll(last, 4, 1).reshape(shape)
    last = last.reshape(shape)
    near = iota((GROUPS // 2, 8, wide), 2) < HEAD_DIM
    upper = iota((GROUPS // 2, 8, wide), 1) < 4
    back_ref[:, 8:16, :] = jnp.where(
        upper,
        jnp.where(near, last[:, 0], turned[:, 0]),
        jnp.where(near, turned[:, 1], last[:, 1]),
    ).astype(BF16)


def finish_kernel(back_ref, row_ref, un_ref, att_ref, guided_ref):
    tokens = row_ref.shape[1]
    rows = back_ref.shape[0]
    wide = 2 * HEAD_DIM
    table = jnp.transpose(row_ref[...])
    row = table.astype(I32).astype(jnp.int16)
    pos = iota((tokens, rows), 1).astype(jnp.int16)
    kept = back_ref[...]
    turned = swap_halves(kept.astype(F32)).astype(BF16)
    left = iota((tokens, wide), 1) < HEAD_DIM
    for j in range(3):
        picks = [one_hot(row[:, h : h + 1] == pos) for h in (2 * j, 2 * j + 1)]
        if j < 2:
            low = matmul(picks[0], turned if j else kept)
            high = matmul(picks[1], kept if j else turned)
        else:
            low, high = matmul(picks[0], kept), matmul(picks[1], kept)
            low = jnp.where(table[:, 6:7] > 0.5, swap_halves(low), low)
            high = jnp.where(table[:, 7:8] > 0.5, high, swap_halves(high))
        att = jnp.where(left, low, high)
        cols = slice(wide * j, wide * (j + 1))
        att_ref[:, cols] = att.astype(BF16)
        un = un_ref[:, cols].astype(F32)
        guided_ref[:, cols] = (un + GUIDE_SCALE * (att - un)).astype(BF16)


def last_kernel(rows_ref, gain_ref, bias_ref, att_ref, c0_ref, c1_ref, c2_ref, *refs):
    outs, buffers, sem = refs[:5], refs[5:9], refs[9]
    copies = []

    def send(ref, out):
        copies.append(pltpu.make_async_copy(ref, out, sem.at[len(copies)]))
        copies[-1].start()

    send(att_ref, outs[1])
    parts, _, width = rows_ref.shape
    total = parts * width
    blocks = [rows_ref[i].astype(F32) for i in range(parts)]
    mean = sum(jnp.sum(b, axis=1, keepdims=True) for b in blocks) * (1.0 / total)
    blocks = [b - mean for b in blocks]
    var = sum(jnp.sum(b * b, axis=1, keepdims=True) for b in blocks) * (1.0 / total)
    scale = lax.rsqrt(var + NORM_EPS)
    for i, b in enumerate(blocks):
        cols = slice(width * i, width * (i + 1))
        buffers[0][:, cols] = (b * scale * gain_ref[:, cols] + bias_ref[:, cols]).astype(BF16)
    send(buffers[0], outs[0])
    first = (att_ref[...].astype(F32) - c0_ref[...].astype(F32)) * 0.5
    buffers[1][...] = first.astype(BF16)
    send(buffers[1], outs[2])
    second = (first - c1_ref[...].astype(F32)) * 0.5
    buffers[2][...] = second.astype(BF16)
    send(buffers[2], outs[3])
    buffers[3][...] = ((second - c2_ref[...].astype(F32)) * 0.5).astype(BF16)
    send(buffers[3], outs[4])
    for copy in copies:
        copy.wait()


VMEM = pl.BlockSpec(memory_space=pltpu.VMEM)
HBM = pl.BlockSpec(memory_space=pl.ANY)
SMEM = pl.BlockSpec(memory_space=pltpu.SMEM)


def in_vmem(x):
    return pltpu.with_memory_space_constraint(x, pltpu.VMEM)


def call(kernel, outs, in_specs, *args, **kw):
    return pl.pallas_call(
        kernel, out_shape=outs, in_specs=in_specs, out_specs=[VMEM] * len(outs), **kw
    )(*args)


def pack(parity, qkv, token_rank, cluster_sizes, cluster_owner, **kw):
    tokens = token_rank.shape[1]
    outs = [pltpu.VMEM((GROUPS, 40, 128), BF16), pltpu.VMEM((8, tokens), F32)]
    scratch = [pltpu.VMEM(qkv.shape, BF16), pltpu.SemaphoreType.DMA]
    args = (parity, qkv, token_rank, cluster_sizes, cluster_owner)
    specs = [SMEM, HBM, VMEM, VMEM, VMEM]
    return call(pack_kernel, outs, specs, *args, scratch_shapes=scratch, **kw)


def attend(arrived, **kw):
    outs = [pltpu.VMEM((GROUPS // 2, 24, 128), BF16)]
    back = call(attend_kernel, outs, [VMEM], in_vmem(arrived), **kw)[0]
    return back.reshape(GROUPS, 3, 4, 128)


def finish(back, table, un, **kw):
    outs = [pltpu.VMEM(un.shape, BF16)] * 2
    args = [in_vmem(x) for x in (back.reshape(GROUPS * 12, 128), table, un)]
    return call(finish_kernel, outs, [VMEM] * 3, *args, **kw)


def last(rows, gain, bias, att, c0, c1, c2, **kw):
    parts, count, width = rows.shape
    shapes = [(count, parts * width)] + [att.shape] * 4
    args = [in_vmem(x) for x in (rows, gain.reshape(1, -1), bias.reshape(1, -1), att, c0, c1, c2)]
    return pl.pallas_call(
        last_kernel,
        out_shape=[jax.ShapeDtypeStruct(s, BF16) for s in shapes],
        in_specs=[VMEM] * 7,
        out_specs=[HBM] * 5,
        scratch_shapes=[pltpu.VMEM(s, BF16) for s in shapes[:1] + shapes[2:]]
        + [pltpu.SemaphoreType.DMA((5,))],
        **kw,
    )(*args)


def on_device(qkv, rank, sizes, owner, c0, c1, c2, un, gain, bias):
    parity = lax.axis_index("tok_2").reshape(1)
    send, table = pack(parity, qkv, rank, sizes, owner)
    arrived = lax.all_to_all(send, TOK, split_axis=0, concat_axis=0, tiled=True)
    back = lax.all_to_all(attend(arrived), TOK, split_axis=0, concat_axis=0, tiled=True)
    att, guided = finish(back, table, un)
    blocks = guided.reshape(8, guided.shape[0] // 8, guided.shape[1])
    rows = lax.all_to_all(blocks, "head", split_axis=0, concat_axis=0, tiled=True)
    return tuple(last(rows, gain, bias, att, c0, c1, c2))


def solution(mesh):
    torus = Mesh(mesh.devices.reshape(4, 8, 2, mesh.shape["head"]), TOK_HEAD)
    in_specs = (
        P(None, TOK, "head"),
        P("head", TOK),
        P("head", None),
        P("head", None),
        P(TOK, "head"),
        P(TOK, "head"),
        P(TOK, "head"),
        P(TOK, "head"),
        P(),
        P(),
    )
    out_specs = (P(TOK_HEAD, None), P(TOK, "head"), P(TOK, "head"), P(TOK, "head"), P(TOK, "head"))
    return jax.shard_map(
        on_device, mesh=torus, in_specs=in_specs, out_specs=out_specs, check_vma=False
    )
```

```python
import math

import jax
import jax.numpy as jnp
from jax import lax
from jax.experimental import pallas as pl
from jax.experimental.pallas import tpu as pltpu
from jax.sharding import PartitionSpec as P

HEAD_DIM = 64
OUT_FIRST, BACK_FIRST, HEAD_FIRST = 45, 45, 5
GROUPS = 64
PAIR_ROWS = 8
MASK_OUT = 32768.0
GUIDE_SCALE = 6.0
NORM_EPS = 1e-05
EXPONENT = math.log2(math.e) / math.sqrt(HEAD_DIM)
F32, BF16, I32 = jnp.float32, jnp.bfloat16, jnp.int32
NT = (((1,), (1,)), ((), ()))


def iota(shape, dim):
    return lax.broadcasted_iota(I32, shape, dim)


def ones_where(cond):
    return jnp.where(cond, 1.0, 0.0).astype(BF16)


def one_hot(cond):
    return jnp.where(cond, jnp.ones(cond.shape, BF16), jnp.zeros(cond.shape, BF16))


def matmul(a, b):
    return jnp.dot(a, b, preferred_element_type=F32)


def swap_halves(x):
    return pltpu.roll(x, HEAD_DIM, 1)


def pack_kernel(
    parity_ref, qkv_hbm, rank_ref, sizes_ref, owner_ref, send_ref, row_ref, qkv_ref, sem
):
    fetch = pltpu.make_async_copy(qkv_hbm, qkv_ref, sem)
    fetch.start()
    heads, tokens = rank_ref.shape
    clusters = sizes_ref.shape[1]
    pairs = heads // 2
    slots = GROUPS * PAIR_ROWS
    before = ones_where(iota((tokens, tokens), 0) < iota((tokens, tokens), 1))
    strict = ones_where(iota((clusters, clusters), 1) < iota((clusters, clusters), 0))
    sizes = sizes_ref[...]
    low = (sizes & 255).astype(F32).astype(BF16)
    high = (sizes >> 8).astype(F32).astype(BF16)
    starts = lax.dot_general(strict, low, NT, preferred_element_type=F32)
    starts = starts + 256.0 * lax.dot_general(strict, high, NT, preferred_element_type=F32)
    owned = [
        jnp.where(iota((GROUPS, clusters), 0) == owner_ref[h : h + 1, :], 1.0, 0.0)
        for h in range(heads)
    ]
    counts = matmul(jnp.concatenate(owned, axis=0).astype(BF16), before)
    first = iota((GROUPS + 8, clusters), 1) == 0
    dests, labels = [], []
    for h in range(heads):
        nth = jnp.sum(owned[h] * counts[GROUPS * h : GROUPS * (h + 1)], axis=0, keepdims=True)
        label = jnp.where(iota((8, clusters), 0) - 4 * (h % 2) == nth.astype(I32), 1.0, 0.0)
        table = jnp.concatenate([owned[h], label], axis=0)
        step = table - jnp.where(first, 0.0, pltpu.roll(table, 1, 1))
        reached = ones_where(starts[:, h : h + 1] <= rank_ref[h : h + 1, :].astype(F32))
        rows = matmul(step.astype(BF16), reached)
        dests.append(rows[:GROUPS])
        labels.append(rows[GROUPS:])
    earlier = matmul(jnp.concatenate(dests, axis=0).astype(BF16), before)
    group_id = iota((GROUPS, 1), 0).astype(F32) * float(PAIR_ROWS)
    slots_iota = iota((slots, tokens), 0).astype(jnp.int16)
    slot_rows, places = [], []
    for h in range(heads):
        offset = group_id
        if h % 2:
            offset = offset + jnp.sum(dests[h - 1], axis=1, keepdims=True)
        ahead = earlier[GROUPS * h : GROUPS * (h + 1)] + offset
        slot = jnp.sum(dests[h] * ahead, axis=0, keepdims=True)
        slot_rows.append(slot)
        places.append(one_hot(slots_iota == slot.astype(I32).astype(jnp.int16)))
    slot = jnp.concatenate(slot_rows, axis=0).astype(I32)
    group, place = ((slot >> 3) + (OUT_FIRST - BACK_FIRST)) & (GROUPS - 1), slot & 7
    mixed_row = 12 * group + 4 * parity_ref[0] + place
    last_row = 12 * group + 8 - 8 * parity_ref[0] + (place & 3)
    back_row = jnp.where(iota(slot.shape, 0) < 4, mixed_row, last_row)
    row_ref[...] = jnp.concatenate([back_row, place[4:6] >> 2], axis=0).astype(F32)
    left = iota((tokens, 2 * HEAD_DIM), 1) < HEAD_DIM
    lane = iota((tokens, 2 * HEAD_DIM), 1)
    marks = []
    for half in range(2):
        zeros = jnp.zeros((HEAD_DIM, tokens), F32)
        rest = jnp.zeros((HEAD_DIM - 8 * pairs, tokens), F32)
        marks.append(jnp.transpose(jnp.concatenate([zeros, *labels[half::2], rest], axis=0)))
    fetch.wait()
    values = []
    for j in range(pairs):
        cols = slice(2 * HEAD_DIM * j, 2 * HEAD_DIM * (j + 1))
        own = (lane >= HEAD_DIM + 8 * j) & (lane < HEAD_DIM + 8 * (j + 1))
        even, odd = (jnp.where(own, m, 0.0) for m in marks)
        q, k, v = (qkv_ref[i, :, cols].astype(F32) for i in range(3))
        qs, ks, vs = swap_halves(q), swap_halves(k), swap_halves(v)
        even = jnp.concatenate([jnp.where(left, q, ks), jnp.where(left, v, even)], axis=1)
        odd = jnp.concatenate([jnp.where(left, qs, k), jnp.where(left, vs, odd)], axis=1)
        place = jnp.concatenate(places[2 * j : 2 * j + 2], axis=1)
        sorted_rows = matmul(place, jnp.concatenate([even, odd], axis=0).astype(BF16))
        send_ref[:, 8 * j : 8 * (j + 1), :] = (
            sorted_rows[:, : 2 * HEAD_DIM].reshape(GROUPS, 8, 2 * HEAD_DIM).astype(BF16)
        )
        values.append(sorted_rows[:, 2 * HEAD_DIM :])
    left = iota((slots, 2 * HEAD_DIM), 1) < HEAD_DIM
    first = jnp.where(left, values[0], swap_halves(values[1]))
    second = jnp.where(left, values[2], values[0] + values[1] + values[2])
    send_ref[:, 24:32, :] = first.reshape(GROUPS, 8, 2 * HEAD_DIM).astype(BF16)
    send_ref[:, 32:40, :] = second.reshape(GROUPS, 8, 2 * HEAD_DIM).astype(BF16)


def put(back_ref, row, value):
    pairs = value.shape[0]
    shift = (OUT_FIRST - BACK_FIRST) // 2 % pairs
    if shift:
        back_ref[shift:, row : row + 8, :] = value[: pairs - shift]
        back_ref[:shift, row : row + 8, :] = value[pairs - shift :]
    else:
        back_ref[:, row : row + 8, :] = value


def attend_kernel(recv_ref, back_ref):
    rows = GROUPS * PAIR_ROWS
    wide = 2 * HEAD_DIM

    def block(k):
        return recv_ref[:, 8 * k : 8 * (k + 1), :].reshape(rows, wide)

    lane = iota((rows, wide), 1)
    left = lane < HEAD_DIM
    values_01 = block(3)
    marks = block(4).astype(F32)
    values_2 = jnp.where(left, marks, swap_halves(marks)).astype(BF16)
    outs = []
    for j in range(3):
        qk = block(j).astype(F32)
        own = (lane >= HEAD_DIM + 8 * j) & (lane < HEAD_DIM + 8 * (j + 1))
        a = jnp.where(left, qk, marks).astype(BF16)
        b = jnp.where(
            left, swap_halves(qk), jnp.where(own, MASK_OUT * (marks - 1.0), 0.0)
        ).astype(BF16)
        scores = lax.dot_general(a, b, NT, preferred_element_type=F32)
        largest = jnp.max(scores, axis=1, keepdims=True)
        expo = jnp.exp2((scores - largest) * EXPONENT)
        totals = jnp.sum(expo, axis=1, keepdims=True)
        probs = (expo * (1.0 / totals)).astype(BF16)
        outs.append(matmul(probs, values_2 if j == 2 else values_01))
    shape = (GROUPS // 2, 2, 8, wide)
    mixed = jnp.where(left, outs[0], outs[1]).reshape(shape).astype(BF16)
    put(back_ref, 0, mixed[:, 0])
    put(back_ref, 16, mixed[:, 1])
    last = outs[2].reshape(GROUPS, 8, wide)
    turned = pltpu.roll(last, 4, 1).reshape(shape)
    last = last.reshape(shape)
    near = iota((GROUPS // 2, 8, wide), 2) < HEAD_DIM
    upper = iota((GROUPS // 2, 8, wide), 1) < 4
    last = jnp.where(
        upper,
        jnp.where(near, last[:, 0], turned[:, 0]),
        jnp.where(near, turned[:, 1], last[:, 1]),
    )
    put(back_ref, 8, last.astype(BF16))


def finish_kernel(back_ref, row_ref, un_ref, att_ref, guided_ref):
    tokens = row_ref.shape[1]
    rows = back_ref.shape[0]
    wide = 2 * HEAD_DIM
    table = jnp.transpose(row_ref[...])
    row = table.astype(I32).astype(jnp.int16)
    pos = iota((tokens, rows), 1).astype(jnp.int16)
    kept = back_ref[...]
    turned = swap_halves(kept.astype(F32)).astype(BF16)
    left = iota((tokens, wide), 1) < HEAD_DIM
    for j in range(3):
        picks = [one_hot(row[:, h : h + 1] == pos) for h in (2 * j, 2 * j + 1)]
        if j < 2:
            low = matmul(picks[0], turned if j else kept)
            high = matmul(picks[1], kept if j else turned)
        else:
            low, high = matmul(picks[0], kept), matmul(picks[1], kept)
            low = jnp.where(table[:, 6:7] > 0.5, swap_halves(low), low)
            high = jnp.where(table[:, 7:8] > 0.5, high, swap_halves(high))
        att = jnp.where(left, low, high)
        cols = slice(wide * j, wide * (j + 1))
        att_ref[:, cols] = att.astype(BF16)
        un = un_ref[:, cols].astype(F32)
        guided = (un + GUIDE_SCALE * (att - un)).astype(BF16)
        parts, count, _ = guided_ref.shape
        for i in range(parts):
            at = (i + HEAD_FIRST) % parts * count
            guided_ref[i, :, cols] = guided[at : at + count]


def last_kernel(rows_ref, gain_ref, bias_ref, att_ref, c0_ref, c1_ref, c2_ref, *refs):
    outs, buffers, sem = refs[:5], refs[5:9], refs[9]
    copies = []

    def send(ref, out):
        copies.append(pltpu.make_async_copy(ref, out, sem.at[len(copies)]))
        copies[-1].start()

    send(att_ref, outs[1])
    parts, _, width = rows_ref.shape
    total = parts * width
    blocks = [rows_ref[i].astype(F32) for i in range(parts)]
    mean = sum(jnp.sum(b, axis=1, keepdims=True) for b in blocks) * (1.0 / total)
    blocks = [b - mean for b in blocks]
    var = sum(jnp.sum(b * b, axis=1, keepdims=True) for b in blocks) * (1.0 / total)
    scale = lax.rsqrt(var + NORM_EPS)
    for i, b in enumerate(blocks):
        at = (i + HEAD_FIRST) % parts
        cols = slice(width * at, width * (at + 1))
        buffers[0][:, cols] = (b * scale * gain_ref[:, cols] + bias_ref[:, cols]).astype(BF16)
    send(buffers[0], outs[0])
    first = (att_ref[...].astype(F32) - c0_ref[...].astype(F32)) * 0.5
    buffers[1][...] = first.astype(BF16)
    send(buffers[1], outs[2])
    second = (first - c1_ref[...].astype(F32)) * 0.5
    buffers[2][...] = second.astype(BF16)
    send(buffers[2], outs[3])
    buffers[3][...] = ((second - c2_ref[...].astype(F32)) * 0.5).astype(BF16)
    send(buffers[3], outs[4])
    for copy in copies:
        copy.wait()


VMEM = pl.BlockSpec(memory_space=pltpu.VMEM)
HBM = pl.BlockSpec(memory_space=pl.ANY)
SMEM = pl.BlockSpec(memory_space=pltpu.SMEM)


def in_vmem(x):
    return pltpu.with_memory_space_constraint(x, pltpu.VMEM)


def call(kernel, outs, in_specs, *args, **kw):
    return pl.pallas_call(
        kernel, out_shape=outs, in_specs=in_specs, out_specs=[VMEM] * len(outs), **kw
    )(*args)


def pack(parity, qkv, token_rank, cluster_sizes, cluster_owner, **kw):
    tokens = token_rank.shape[1]
    outs = [pltpu.VMEM((GROUPS, 40, 128), BF16), pltpu.VMEM((8, tokens), F32)]
    scratch = [pltpu.VMEM(qkv.shape, BF16), pltpu.SemaphoreType.DMA]
    args = (parity, qkv, token_rank, cluster_sizes, cluster_owner)
    specs = [SMEM, HBM, VMEM, VMEM, VMEM]
    return call(pack_kernel, outs, specs, *args, scratch_shapes=scratch, **kw)


def attend(arrived, **kw):
    outs = [pltpu.VMEM((GROUPS // 2, 24, 128), BF16)]
    back = call(attend_kernel, outs, [VMEM], in_vmem(arrived), **kw)[0]
    return back.reshape(GROUPS, 3, 4, 128)


def finish(back, table, un, **kw):
    outs = [pltpu.VMEM(un.shape, BF16), pltpu.VMEM((8, un.shape[0] // 8, un.shape[1]), BF16)]
    args = [in_vmem(x) for x in (back.reshape(GROUPS * 12, 128), table, un)]
    return call(finish_kernel, outs, [VMEM] * 3, *args, **kw)


def last(rows, gain, bias, att, c0, c1, c2, **kw):
    parts, count, width = rows.shape
    shapes = [(count, parts * width)] + [att.shape] * 4
    args = [in_vmem(x) for x in (rows, gain.reshape(1, -1), bias.reshape(1, -1), att, c0, c1, c2)]
    return pl.pallas_call(
        last_kernel,
        out_shape=[jax.ShapeDtypeStruct(s, BF16) for s in shapes],
        in_specs=[VMEM] * 7,
        out_specs=[HBM] * 5,
        scratch_shapes=[pltpu.VMEM(s, BF16) for s in shapes[:1] + shapes[2:]]
        + [pltpu.SemaphoreType.DMA((5,))],
        **kw,
    )(*args)


def exchange(x, axis, first):
    size = lax.axis_size(axis)
    order = [[(first + i) % size for i in range(size)]]
    return lax.all_to_all(x, axis, 0, 0, axis_index_groups=order, tiled=True)


def on_device(qkv, rank, sizes, owner, c0, c1, c2, un, gain, bias):
    parity = ((lax.axis_index("tok") + BACK_FIRST) % 2).reshape(1)
    send, table = pack(parity, qkv, rank, sizes, owner)
    arrived = exchange(send, "tok", OUT_FIRST)
    back = exchange(attend(arrived), "tok", BACK_FIRST)
    att, guided = finish(back, table, un)
    rows = exchange(guided, "head", HEAD_FIRST)
    return tuple(last(rows, gain, bias, att, c0, c1, c2))


def solution(mesh):
    cached = P("tok", "head")
    in_specs = (P(None, "tok", "head"), P("head", "tok"), P("head", None), P("head", None))
    in_specs = in_specs + (cached,) * 4 + (P(), P())
    out_specs = (P(("tok", "head"), None),) + (cached,) * 4
    return jax.shard_map(
        on_device, mesh=mesh, in_specs=in_specs, out_specs=out_specs, check_vma=False
    )
```

```python
import math

import jax
import jax.numpy as jnp
from jax import lax
from jax.experimental import pallas as pl
from jax.experimental.pallas import tpu as pltpu
from jax.sharding import PartitionSpec as P

HEAD_DIM = 64
TOK_ORDER = [
    (16 * (x % 4)) + 2 * (z % 8) + core for core in (1, 0) for z in range(6, 14) for x in range(2, 6)
]
HEAD_ORDER = [5, 1, 6, 2, 7, 3, 0, 4]
GROUPS = 64
PAIR_ROWS = 8
MASK_OUT = 32768.0
GUIDE_SCALE = 6.0
NORM_EPS = 1e-05
EXPONENT = math.log2(math.e) / math.sqrt(HEAD_DIM)
F32, BF16, I32 = jnp.float32, jnp.bfloat16, jnp.int32
NT = (((1,), (1,)), ((), ()))


def iota(shape, dim):
    return lax.broadcasted_iota(I32, shape, dim)


def ones_where(cond):
    return jnp.where(cond, 1.0, 0.0).astype(BF16)


def one_hot(cond):
    return jnp.where(cond, jnp.ones(cond.shape, BF16), jnp.zeros(cond.shape, BF16))


def matmul(a, b):
    return jnp.dot(a, b, preferred_element_type=F32)


def swap_halves(x):
    return pltpu.roll(x, HEAD_DIM, 1)


def pack_kernel(
    parity_ref,
    qkv_hbm,
    rank_hbm,
    sizes_hbm,
    owner_hbm,
    send_ref,
    row_ref,
    sizes_ref,
    owner_ref,
    rank_ref,
    qkv_ref,
    sem,
):
    sources = (sizes_hbm, owner_hbm, rank_hbm, qkv_hbm)
    targets = (sizes_ref, owner_ref, rank_ref, qkv_ref)
    fetches = [
        pltpu.make_async_copy(src, dst, sem.at[i])
        for i, (src, dst) in enumerate(zip(sources, targets))
    ]
    for fetch in fetches:
        fetch.start()
    heads, tokens = rank_ref.shape
    clusters = sizes_ref.shape[1]
    pairs = heads // 2
    slots = GROUPS * PAIR_ROWS
    before = ones_where(iota((tokens, tokens), 0) < iota((tokens, tokens), 1))
    strict = ones_where(iota((clusters, clusters), 1) < iota((clusters, clusters), 0))
    slots_iota = iota((slots, tokens), 0).astype(jnp.int16)
    for fetch in fetches[:3]:
        fetch.wait()
    sizes = sizes_ref[...]
    low = (sizes & 255).astype(F32).astype(BF16)
    high = (sizes >> 8).astype(F32).astype(BF16)
    starts = lax.dot_general(strict, low, NT, preferred_element_type=F32)
    starts = starts + 256.0 * lax.dot_general(strict, high, NT, preferred_element_type=F32)
    owned = [
        jnp.where(iota((GROUPS, clusters), 0) == owner_ref[h : h + 1, :], 1.0, 0.0)
        for h in range(heads)
    ]
    counts = matmul(jnp.concatenate(owned, axis=0).astype(BF16), before)
    first = iota((GROUPS + 8, clusters), 1) == 0
    dests, labels = [], []
    for h in range(heads):
        nth = jnp.sum(owned[h] * counts[GROUPS * h : GROUPS * (h + 1)], axis=0, keepdims=True)
        label = jnp.where(iota((8, clusters), 0) - 4 * (h % 2) == nth.astype(I32), 1.0, 0.0)
        table = jnp.concatenate([owned[h], label], axis=0)
        step = table - jnp.where(first, 0.0, pltpu.roll(table, 1, 1))
        reached = ones_where(starts[:, h : h + 1] <= rank_ref[h : h + 1, :].astype(F32))
        rows = matmul(step.astype(BF16), reached)
        dests.append(rows[:GROUPS])
        labels.append(rows[GROUPS:])
    earlier = matmul(jnp.concatenate(dests, axis=0).astype(BF16), before)
    group_id = iota((GROUPS, 1), 0).astype(F32) * float(PAIR_ROWS)
    slot_rows, places = [], []
    for h in range(heads):
        offset = group_id
        if h % 2:
            offset = offset + jnp.sum(dests[h - 1], axis=1, keepdims=True)
        ahead = earlier[GROUPS * h : GROUPS * (h + 1)] + offset
        slot = jnp.sum(dests[h] * ahead, axis=0, keepdims=True)
        slot_rows.append(slot)
        places.append(one_hot(slots_iota == slot.astype(I32).astype(jnp.int16)))
    slot = jnp.concatenate(slot_rows, axis=0).astype(I32)
    group, place = slot >> 3, slot & 7
    mixed_row = 12 * group + 4 * parity_ref[0] + place
    last_row = 12 * group + 8 - 8 * parity_ref[0] + (place & 3)
    back_row = jnp.where(iota(slot.shape, 0) < 4, mixed_row, last_row)
    row_ref[...] = jnp.concatenate([back_row, place[4:6] >> 2], axis=0).astype(F32)
    left = iota((tokens, 2 * HEAD_DIM), 1) < HEAD_DIM
    lane = iota((tokens, 2 * HEAD_DIM), 1)
    marks = []
    for half in range(2):
        zeros = jnp.zeros((HEAD_DIM, tokens), F32)
        rest = jnp.zeros((HEAD_DIM - 8 * pairs, tokens), F32)
        marks.append(jnp.transpose(jnp.concatenate([zeros, *labels[half::2], rest], axis=0)))
    fetches[3].wait()
    values = []
    for j in range(pairs):
        cols = slice(2 * HEAD_DIM * j, 2 * HEAD_DIM * (j + 1))
        own = (lane >= HEAD_DIM + 8 * j) & (lane < HEAD_DIM + 8 * (j + 1))
        even, odd = (jnp.where(own, m, 0.0) for m in marks)
        q, k, v = (qkv_ref[i, :, cols].astype(F32) for i in range(3))
        qs, ks, vs = swap_halves(q), swap_halves(k), swap_halves(v)
        even = jnp.concatenate([jnp.where(left, q, ks), jnp.where(left, v, even)], axis=1)
        odd = jnp.concatenate([jnp.where(left, qs, k), jnp.where(left, vs, odd)], axis=1)
        place = jnp.concatenate(places[2 * j : 2 * j + 2], axis=1)
        sorted_rows = matmul(place, jnp.concatenate([even, odd], axis=0).astype(BF16))
        send_ref[:, 8 * j : 8 * (j + 1), :] = (
            sorted_rows[:, : 2 * HEAD_DIM].reshape(GROUPS, 8, 2 * HEAD_DIM).astype(BF16)
        )
        values.append(sorted_rows[:, 2 * HEAD_DIM :])
    left = iota((slots, 2 * HEAD_DIM), 1) < HEAD_DIM
    first = jnp.where(left, values[0], swap_halves(values[1]))
    second = jnp.where(left, values[2], values[0] + values[1] + values[2])
    send_ref[:, 24:32, :] = first.reshape(GROUPS, 8, 2 * HEAD_DIM).astype(BF16)
    send_ref[:, 32:40, :] = second.reshape(GROUPS, 8, 2 * HEAD_DIM).astype(BF16)


def attend_kernel(recv_ref, back_ref):
    rows = GROUPS * PAIR_ROWS
    wide = 2 * HEAD_DIM

    def block(k):
        return recv_ref[:, 8 * k : 8 * (k + 1), :].reshape(rows, wide)

    lane = iota((rows, wide), 1)
    left = lane < HEAD_DIM
    values_01 = block(3)
    marks = block(4).astype(F32)
    values_2 = jnp.where(left, marks, swap_halves(marks)).astype(BF16)

    def operands(j):
        qk = block(j).astype(F32)
        own = (lane >= HEAD_DIM + 8 * j) & (lane < HEAD_DIM + 8 * (j + 1))
        a = jnp.where(left, qk, marks).astype(BF16)
        b = jnp.where(
            left, swap_halves(qk), jnp.where(own, MASK_OUT * (marks - 1.0), 0.0)
        ).astype(BF16)
        return a, b

    def score(ab):
        return lax.dot_general(ab[0], ab[1], NT, preferred_element_type=F32)

    def softmax(scores):
        largest = jnp.max(scores, axis=1, keepdims=True)
        expo = jnp.exp2((scores - largest) * EXPONENT)
        totals = jnp.sum(expo, axis=1, keepdims=True)
        return (expo * (1.0 / totals)).astype(BF16)

    ab = [operands(j) for j in range(3)]
    scores = [score(x) for x in ab]
    probs = [softmax(x) for x in scores]
    outs = [matmul(p, values_2 if j == 2 else values_01) for j, p in enumerate(probs)]
    shape = (GROUPS // 2, 2, 8, wide)
    mixed = jnp.where(left, outs[0], outs[1]).reshape(shape).astype(BF16)
    back_ref[:, 0:8, :] = mixed[:, 0]
    back_ref[:, 16:24, :] = mixed[:, 1]
    last = outs[2].reshape(GROUPS, 8, wide)
    turned = pltpu.roll(last, 4, 1).reshape(shape)
    last = last.reshape(shape)
    near = iota((GROUPS // 2, 8, wide), 2) < HEAD_DIM
    upper = iota((GROUPS // 2, 8, wide), 1) < 4
    last = jnp.where(
        upper,
        jnp.where(near, last[:, 0], turned[:, 0]),
        jnp.where(near, turned[:, 1], last[:, 1]),
    )
    back_ref[:, 8:16, :] = last.astype(BF16)


def finish_kernel(back_ref, row_ref, un_ref, att_ref, guided_ref):
    tokens = row_ref.shape[1]
    rows = back_ref.shape[0]
    wide = 2 * HEAD_DIM
    table = jnp.transpose(row_ref[...])
    row = table.astype(I32).astype(jnp.int16)
    pos = iota((tokens, rows), 1).astype(jnp.int16)
    kept = back_ref[...]
    left = iota((tokens, wide), 1) < HEAD_DIM
    for j in range(3):
        low, high = (matmul(one_hot(row[:, h : h + 1] == pos), kept) for h in (2 * j, 2 * j + 1))
        if j == 0:
            high = swap_halves(high)
        elif j == 1:
            low = swap_halves(low)
        else:
            low = jnp.where(table[:, 6:7] > 0.5, swap_halves(low), low)
            high = jnp.where(table[:, 7:8] > 0.5, high, swap_halves(high))
        att = jnp.where(left, low, high)
        cols = slice(wide * j, wide * (j + 1))
        att_ref[:, cols] = att.astype(BF16)
        un = un_ref[:, cols].astype(F32)
        guided = (un + GUIDE_SCALE * (att - un)).astype(BF16)
        parts, count, _ = guided_ref.shape
        for i in range(parts):
            at = HEAD_ORDER[i] * count
            guided_ref[i, :, cols] = guided[at : at + count]


def last_kernel(rows_ref, gain_ref, bias_ref, att_ref, c0_ref, c1_ref, c2_ref, *refs):
    outs, buffers, sem = refs[:5], refs[5:9], refs[9]
    copies = []

    def send(ref, out):
        copies.append(pltpu.make_async_copy(ref, out, sem.at[len(copies)]))
        copies[-1].start()

    send(att_ref, outs[1])
    parts, _, width = rows_ref.shape
    total = parts * width
    blocks = [rows_ref[i].astype(F32) for i in range(parts)]
    mean = sum(jnp.sum(b, axis=1, keepdims=True) for b in blocks) * (1.0 / total)
    blocks = [b - mean for b in blocks]
    var = sum(jnp.sum(b * b, axis=1, keepdims=True) for b in blocks) * (1.0 / total)
    scale = lax.rsqrt(var + NORM_EPS)
    for i, b in enumerate(blocks):
        cols = slice(width * HEAD_ORDER[i], width * (HEAD_ORDER[i] + 1))
        buffers[0][:, cols] = (b * scale * gain_ref[:, cols] + bias_ref[:, cols]).astype(BF16)
    send(buffers[0], outs[0])
    chunk = att_ref.shape[0] // 4
    for start in range(0, att_ref.shape[0], chunk):
        rows = slice(start, start + chunk)
        first = (att_ref[rows].astype(F32) - c0_ref[rows].astype(F32)) * 0.5
        second = (first - c1_ref[rows].astype(F32)) * 0.5
        third = (second - c2_ref[rows].astype(F32)) * 0.5
        for i, term in enumerate((first, second, third)):
            buffers[1 + i][rows] = term.astype(BF16)
    for i in range(3):
        send(buffers[1 + i], outs[2 + i])
    for copy in copies:
        copy.wait()


VMEM = pl.BlockSpec(memory_space=pltpu.VMEM)
HBM = pl.BlockSpec(memory_space=pl.ANY)
SMEM = pl.BlockSpec(memory_space=pltpu.SMEM)


def in_vmem(x):
    return pltpu.with_memory_space_constraint(x, pltpu.VMEM)


def call(kernel, outs, in_specs, *args, **kw):
    return pl.pallas_call(
        kernel, out_shape=outs, in_specs=in_specs, out_specs=[VMEM] * len(outs), **kw
    )(*args)


def pack(parity, qkv, token_rank, cluster_sizes, cluster_owner, **kw):
    tokens = token_rank.shape[1]
    outs = [pltpu.VMEM((GROUPS, 40, 128), BF16), pltpu.VMEM((8, tokens), F32)]
    scratch = [pltpu.VMEM(x.shape, x.dtype) for x in (cluster_sizes, cluster_owner, token_rank, qkv)]
    scratch.append(pltpu.SemaphoreType.DMA((4,)))
    args = (parity, qkv, token_rank, cluster_sizes, cluster_owner)
    specs = [SMEM, HBM, HBM, HBM, HBM]
    return call(pack_kernel, outs, specs, *args, scratch_shapes=scratch, **kw)


def attend(arrived, **kw):
    outs = [pltpu.VMEM((GROUPS // 2, 24, 128), BF16)]
    back = call(attend_kernel, outs, [VMEM], in_vmem(arrived), **kw)[0]
    return back.reshape(GROUPS, 3, 4, 128)


def finish(back, table, un, **kw):
    outs = [pltpu.VMEM(un.shape, BF16), pltpu.VMEM((8, un.shape[0] // 8, un.shape[1]), BF16)]
    args = [in_vmem(x) for x in (back.reshape(GROUPS * 12, 128), table, un)]
    return call(finish_kernel, outs, [VMEM] * 3, *args, **kw)


def last(rows, gain, bias, att, c0, c1, c2, **kw):
    parts, count, width = rows.shape
    shapes = [(count, parts * width)] + [att.shape] * 4
    args = [in_vmem(x) for x in (rows, gain.reshape(1, -1), bias.reshape(1, -1), att, c0, c1, c2)]
    return pl.pallas_call(
        last_kernel,
        out_shape=[jax.ShapeDtypeStruct(s, BF16) for s in shapes],
        in_specs=[VMEM] * 7,
        out_specs=[HBM] * 5,
        scratch_shapes=[pltpu.VMEM(s, BF16) for s in shapes[:1] + shapes[2:]]
        + [pltpu.SemaphoreType.DMA((5,))],
        **kw,
    )(*args)


def exchange(x, axis, order):
    return lax.all_to_all(x, axis, 0, 0, axis_index_groups=[order], tiled=True)


def on_device(qkv, rank, sizes, owner, c0, c1, c2, un, gain, bias):
    parity = ((lax.axis_index("tok") >> 4) & 1).reshape(1)
    send, table = pack(parity, qkv, rank, sizes, owner)
    arrived = exchange(send, "tok", TOK_ORDER)
    back = exchange(attend(arrived), "tok", TOK_ORDER)
    att, guided = finish(back, table, un)
    rows = exchange(guided, "head", HEAD_ORDER)
    return tuple(last(rows, gain, bias, att, c0, c1, c2))


def solution(mesh):
    cached = P("tok", "head")
    in_specs = (P(None, "tok", "head"), P("head", "tok"), P("head", None), P("head", None))
    in_specs = in_specs + (cached,) * 4 + (P(), P())
    out_specs = (P(("tok", "head"), None),) + (cached,) * 4
    return jax.shard_map(
        on_device, mesh=mesh, in_specs=in_specs, out_specs=out_specs, check_vma=False
    )
```

```python
import math

import jax
import jax.numpy as jnp
from jax import lax
from jax.experimental import pallas as pl
from jax.experimental.pallas import tpu as pltpu
from jax.sharding import PartitionSpec as P

HEAD_DIM = 64
TOK_ORDER = [
    (16 * (x % 4)) + 2 * (z % 8) + core for core in (1, 0) for z in range(6, 14) for x in range(2, 6)
]
HEAD_ORDER = [5, 1, 6, 2, 7, 3, 0, 4]
GROUPS = 64
PAIR_ROWS = 8
MASK_OUT = 32768.0
GUIDE_SCALE = 6.0
NORM_EPS = 1e-05
EXPONENT = math.log2(math.e) / math.sqrt(HEAD_DIM)
F32, BF16, I32 = jnp.float32, jnp.bfloat16, jnp.int32
NT = (((1,), (1,)), ((), ()))


def iota(shape, dim):
    return lax.broadcasted_iota(I32, shape, dim)


def ones_where(cond):
    return jnp.where(cond, 1.0, 0.0).astype(BF16)


def one_hot(cond):
    return jnp.where(cond, jnp.ones(cond.shape, BF16), jnp.zeros(cond.shape, BF16))


def matmul(a, b):
    return jnp.dot(a, b, preferred_element_type=F32)


def swap_halves(x):
    return pltpu.roll(x, HEAD_DIM, 1)


def pack_kernel(
    parity_ref,
    qkv_hbm,
    rank_hbm,
    sizes_hbm,
    owner_hbm,
    send_ref,
    row_ref,
    sizes_ref,
    owner_ref,
    rank_ref,
    qkv_ref,
    sem,
):
    sources = (sizes_hbm, owner_hbm, rank_hbm, qkv_hbm)
    targets = (sizes_ref, owner_ref, rank_ref, qkv_ref)
    fetches = [
        pltpu.make_async_copy(src, dst, sem.at[i])
        for i, (src, dst) in enumerate(zip(sources, targets))
    ]
    for fetch in fetches:
        fetch.start()
    heads, tokens = rank_ref.shape
    clusters = sizes_ref.shape[1]
    pairs = heads // 2
    slots = GROUPS * PAIR_ROWS
    before = ones_where(iota((tokens, tokens), 0) < iota((tokens, tokens), 1))
    strict = ones_where(iota((clusters, clusters), 1) < iota((clusters, clusters), 0))
    slots_iota = iota((slots, tokens), 0).astype(jnp.int16)
    for fetch in fetches[:3]:
        fetch.wait()
    sizes = sizes_ref[...]
    low = (sizes & 255).astype(F32).astype(BF16)
    high = (sizes >> 8).astype(F32).astype(BF16)
    starts = lax.dot_general(strict, low, NT, preferred_element_type=F32)
    starts = starts + 256.0 * lax.dot_general(strict, high, NT, preferred_element_type=F32)
    starts = starts.astype(I32).astype(jnp.int16)
    ranks = rank_ref[...].astype(jnp.int16)
    owned = [
        jnp.where(iota((GROUPS, clusters), 0) == owner_ref[h : h + 1, :], 1.0, 0.0)
        for h in range(heads)
    ]
    counts = matmul(jnp.concatenate(owned, axis=0).astype(BF16), before)
    first = iota((GROUPS + 8, clusters), 1) == 0
    dests, labels = [], []
    for h in range(heads):
        nth = jnp.sum(owned[h] * counts[GROUPS * h : GROUPS * (h + 1)], axis=0, keepdims=True)
        label = jnp.where(iota((8, clusters), 0) - 4 * (h % 2) == nth.astype(I32), 1.0, 0.0)
        table = jnp.concatenate([owned[h], label], axis=0)
        step = table - jnp.where(first, 0.0, pltpu.roll(table, 1, 1))
        reached = one_hot(starts[:, h : h + 1] <= ranks[h : h + 1, :])
        rows = matmul(step.astype(BF16), reached)
        dests.append(rows[:GROUPS])
        labels.append(rows[GROUPS:])
    earlier = matmul(jnp.concatenate(dests, axis=0).astype(BF16), before)
    group_id = iota((GROUPS, 1), 0).astype(F32) * float(PAIR_ROWS)
    slot_rows, places = [], []
    for h in range(heads):
        offset = group_id
        if h % 2:
            offset = offset + jnp.sum(dests[h - 1], axis=1, keepdims=True)
        ahead = earlier[GROUPS * h : GROUPS * (h + 1)] + offset
        slot = jnp.sum(dests[h] * ahead, axis=0, keepdims=True)
        slot_rows.append(slot)
        places.append(one_hot(slots_iota == slot.astype(I32).astype(jnp.int16)))
    slot = jnp.concatenate(slot_rows, axis=0).astype(I32)
    group, place = slot >> 3, slot & 7
    mixed_row = 12 * group + 4 * parity_ref[0] + place
    last_row = 12 * group + 8 - 8 * parity_ref[0] + (place & 3)
    back_row = jnp.where(iota(slot.shape, 0) < 4, mixed_row, last_row)
    row_ref[...] = jnp.concatenate([back_row, place[4:6] >> 2], axis=0).astype(F32)
    left = iota((tokens, 2 * HEAD_DIM), 1) < HEAD_DIM
    lane = iota((tokens, 2 * HEAD_DIM), 1)
    marks = []
    for half in range(2):
        zeros = jnp.zeros((HEAD_DIM, tokens), F32)
        rest = jnp.zeros((HEAD_DIM - 8 * pairs, tokens), F32)
        marks.append(jnp.transpose(jnp.concatenate([zeros, *labels[half::2], rest], axis=0)))
    fetches[3].wait()
    values = []
    for j in range(pairs):
        cols = slice(2 * HEAD_DIM * j, 2 * HEAD_DIM * (j + 1))
        own = (lane >= HEAD_DIM + 8 * j) & (lane < HEAD_DIM + 8 * (j + 1))
        even, odd = (jnp.where(own, m, 0.0) for m in marks)
        q, k, v = (qkv_ref[i, :, cols].astype(F32) for i in range(3))
        qs, ks, vs = swap_halves(q), swap_halves(k), swap_halves(v)
        even = jnp.concatenate([jnp.where(left, q, ks), jnp.where(left, v, even)], axis=1)
        odd = jnp.concatenate([jnp.where(left, qs, k), jnp.where(left, vs, odd)], axis=1)
        place = jnp.concatenate(places[2 * j : 2 * j + 2], axis=1)
        sorted_rows = matmul(place, jnp.concatenate([even, odd], axis=0).astype(BF16))
        send_ref[:, 8 * j : 8 * (j + 1), :] = (
            sorted_rows[:, : 2 * HEAD_DIM].reshape(GROUPS, 8, 2 * HEAD_DIM).astype(BF16)
        )
        values.append(sorted_rows[:, 2 * HEAD_DIM :])
    left = iota((slots, 2 * HEAD_DIM), 1) < HEAD_DIM
    first = jnp.where(left, values[0], swap_halves(values[1]))
    second = jnp.where(left, values[2], values[0] + values[1] + values[2])
    send_ref[:, 24:32, :] = first.reshape(GROUPS, 8, 2 * HEAD_DIM).astype(BF16)
    send_ref[:, 32:40, :] = second.reshape(GROUPS, 8, 2 * HEAD_DIM).astype(BF16)


def attend_kernel(recv_ref, back_ref):
    rows = GROUPS * PAIR_ROWS
    wide = 2 * HEAD_DIM

    def block(k):
        return recv_ref[:, 8 * k : 8 * (k + 1), :].reshape(rows, wide)

    lane = iota((rows, wide), 1)
    left = lane < HEAD_DIM
    values_01 = block(3)
    marks = block(4).astype(F32)
    values_2 = jnp.where(left, marks, swap_halves(marks)).astype(BF16)

    def operands(j):
        qk = block(j).astype(F32)
        own = (lane >= HEAD_DIM + 8 * j) & (lane < HEAD_DIM + 8 * (j + 1))
        a = jnp.where(left, qk, marks).astype(BF16)
        b = jnp.where(
            left, swap_halves(qk), jnp.where(own, MASK_OUT * (marks - 1.0), 0.0)
        ).astype(BF16)
        return a, b

    def score(ab):
        return lax.dot_general(ab[0], ab[1], NT, preferred_element_type=F32)

    def softmax(scores):
        largest = jnp.max(scores, axis=1, keepdims=True)
        expo = jnp.exp2((scores - largest) * EXPONENT)
        totals = jnp.sum(expo, axis=1, keepdims=True)
        return (expo * (1.0 / totals)).astype(BF16)

    ab = [operands(j) for j in range(3)]
    scores = [score(x) for x in ab]
    probs = [softmax(x) for x in scores]
    outs = [matmul(p, values_2 if j == 2 else values_01) for j, p in enumerate(probs)]
    shape = (GROUPS // 2, 2, 8, wide)
    mixed = jnp.where(left, outs[0], outs[1]).reshape(shape).astype(BF16)
    back_ref[:, 0:8, :] = mixed[:, 0]
    back_ref[:, 16:24, :] = mixed[:, 1]
    last = outs[2].reshape(GROUPS, 8, wide)
    turned = pltpu.roll(last, 4, 1).reshape(shape)
    last = last.reshape(shape)
    near = iota((GROUPS // 2, 8, wide), 2) < HEAD_DIM
    upper = iota((GROUPS // 2, 8, wide), 1) < 4
    last = jnp.where(
        upper,
        jnp.where(near, last[:, 0], turned[:, 0]),
        jnp.where(near, turned[:, 1], last[:, 1]),
    )
    back_ref[:, 8:16, :] = last.astype(BF16)


def finish_kernel(parity_ref, back_ref, row_ref, un_ref, att_ref, guided_ref):
    tokens = row_ref.shape[1]
    rows = back_ref.shape[0]
    wide = 2 * HEAD_DIM
    table = jnp.transpose(row_ref[...])
    row = table.astype(I32).astype(jnp.int16)
    pos = iota((tokens, rows), 1).astype(jnp.int16)
    kept = back_ref[...]
    quarter = iota((rows // 24, 24, wide), 1) >> 2
    own = quarter == 2 - 2 * parity_ref[0]
    own = (own | (quarter == 5 - 2 * parity_ref[0])).reshape(rows, wide)
    apart = kept.astype(F32)
    apart = jnp.concatenate([jnp.where(own, 0.0, apart), jnp.where(own, apart, 0.0)], axis=1)
    apart = apart.astype(BF16)
    left = iota((tokens, wide), 1) < HEAD_DIM
    hits = [row[:, h : h + 1] == pos for h in range(6)]
    both = [matmul(one_hot(hits[h] | hits[h + 4]), apart) for h in range(2)]
    found = [x[:, :wide] for x in both] + [matmul(one_hot(hits[h]), kept) for h in (2, 3)]
    found += [x[:, wide:] for x in both]
    for j in range(3):
        low, high = found[2 * j], found[2 * j + 1]
        if j == 0:
            high = swap_halves(high)
        elif j == 1:
            low = swap_halves(low)
        else:
            low = jnp.where(table[:, 6:7] > 0.5, swap_halves(low), low)
            high = jnp.where(table[:, 7:8] > 0.5, high, swap_halves(high))
        att = jnp.where(left, low, high)
        cols = slice(wide * j, wide * (j + 1))
        att_ref[:, cols] = att.astype(BF16)
        un = un_ref[:, cols].astype(F32)
        guided = (un + GUIDE_SCALE * (att - un)).astype(BF16)
        parts, count, _ = guided_ref.shape
        for i in range(parts):
            at = HEAD_ORDER[i] * count
            guided_ref[i, :, cols] = guided[at : at + count]


def last_kernel(rows_ref, gain_ref, bias_ref, att_ref, c0_ref, c1_ref, c2_ref, *refs):
    outs, buffers, sem = refs[:5], refs[5:9], refs[9]
    copies = []

    def send(ref, out):
        copies.append(pltpu.make_async_copy(ref, out, sem.at[len(copies)]))
        copies[-1].start()

    send(att_ref, outs[1])
    chunk = att_ref.shape[0] // 4
    for start in range(0, att_ref.shape[0], chunk):
        rows = slice(start, start + chunk)
        first = (att_ref[rows].astype(F32) - c0_ref[rows].astype(F32)) * 0.5
        second = (first - c1_ref[rows].astype(F32)) * 0.5
        third = (second - c2_ref[rows].astype(F32)) * 0.5
        for i, term in enumerate((first, second, third)):
            buffers[1 + i][rows] = term.astype(BF16)
    for i in range(3):
        send(buffers[1 + i], outs[2 + i])
    parts, _, width = rows_ref.shape
    total = parts * width
    blocks = [rows_ref[i].astype(F32) for i in range(parts)]
    mean = sum(jnp.sum(b, axis=1, keepdims=True) for b in blocks) * (1.0 / total)
    blocks = [b - mean for b in blocks]
    var = sum(jnp.sum(b * b, axis=1, keepdims=True) for b in blocks) * (1.0 / total)
    scale = lax.rsqrt(var + NORM_EPS)
    for i, b in enumerate(blocks):
        cols = slice(width * HEAD_ORDER[i], width * (HEAD_ORDER[i] + 1))
        buffers[0][:, cols] = (b * scale * gain_ref[:, cols] + bias_ref[:, cols]).astype(BF16)
    send(buffers[0], outs[0])
    for copy in copies:
        copy.wait()


VMEM = pl.BlockSpec(memory_space=pltpu.VMEM)
HBM = pl.BlockSpec(memory_space=pl.ANY)
SMEM = pl.BlockSpec(memory_space=pltpu.SMEM)


def in_vmem(x):
    return pltpu.with_memory_space_constraint(x, pltpu.VMEM)


def call(kernel, outs, in_specs, *args, **kw):
    return pl.pallas_call(
        kernel, out_shape=outs, in_specs=in_specs, out_specs=[VMEM] * len(outs), **kw
    )(*args)


def pack(parity, qkv, token_rank, cluster_sizes, cluster_owner, **kw):
    tokens = token_rank.shape[1]
    outs = [pltpu.VMEM((GROUPS, 40, 128), BF16), pltpu.VMEM((8, tokens), F32)]
    scratch = [pltpu.VMEM(x.shape, x.dtype) for x in (cluster_sizes, cluster_owner, token_rank, qkv)]
    scratch.append(pltpu.SemaphoreType.DMA((4,)))
    args = (parity, qkv, token_rank, cluster_sizes, cluster_owner)
    specs = [SMEM, HBM, HBM, HBM, HBM]
    return call(pack_kernel, outs, specs, *args, scratch_shapes=scratch, **kw)


def attend(arrived, **kw):
    outs = [pltpu.VMEM((GROUPS // 2, 24, 128), BF16)]
    back = call(attend_kernel, outs, [VMEM], in_vmem(arrived), **kw)[0]
    return back.reshape(GROUPS, 3, 4, 128)


def finish(parity, back, table, un, **kw):
    outs = [pltpu.VMEM(un.shape, BF16), pltpu.VMEM((8, un.shape[0] // 8, un.shape[1]), BF16)]
    args = [in_vmem(x) for x in (back.reshape(GROUPS * 12, 128), table, un)]
    return call(finish_kernel, outs, [SMEM] + [VMEM] * 3, parity, *args, **kw)


def last(rows, gain, bias, att, c0, c1, c2, **kw):
    parts, count, width = rows.shape
    shapes = [(count, parts * width)] + [att.shape] * 4
    args = [in_vmem(x) for x in (rows, gain.reshape(1, -1), bias.reshape(1, -1), att, c0, c1, c2)]
    return pl.pallas_call(
        last_kernel,
        out_shape=[jax.ShapeDtypeStruct(s, BF16) for s in shapes],
        in_specs=[VMEM] * 7,
        out_specs=[HBM] * 5,
        scratch_shapes=[pltpu.VMEM(s, BF16) for s in shapes[:1] + shapes[2:]]
        + [pltpu.SemaphoreType.DMA((5,))],
        **kw,
    )(*args)


def exchange(x, axis, order):
    return lax.all_to_all(x, axis, 0, 0, axis_index_groups=[order], tiled=True)


def on_device(qkv, rank, sizes, owner, c0, c1, c2, un, gain, bias):
    parity = ((lax.axis_index("tok") >> 4) & 1).reshape(1)
    send, table = pack(parity, qkv, rank, sizes, owner)
    arrived = exchange(send, "tok", TOK_ORDER)
    back = exchange(attend(arrived), "tok", TOK_ORDER)
    att, guided = finish(parity, back, table, un)
    rows = exchange(guided, "head", HEAD_ORDER)
    return tuple(last(rows, gain, bias, att, c0, c1, c2))


def solution(mesh):
    cached = P("tok", "head")
    in_specs = (P(None, "tok", "head"), P("head", "tok"), P("head", None), P("head", None))
    in_specs = in_specs + (cached,) * 4 + (P(), P())
    out_specs = (P(("tok", "head"), None),) + (cached,) * 4
    return jax.shard_map(
        on_device, mesh=mesh, in_specs=in_specs, out_specs=out_specs, check_vma=False
    )
```

```python
import math

import jax
import jax.numpy as jnp
from jax import lax
from jax.experimental import pallas as pl
from jax.experimental.pallas import tpu as pltpu
from jax.sharding import PartitionSpec as P

HEAD_DIM = 64
TOK_ORDER = [
    (16 * (x % 4)) + 2 * (z % 8) + core for core in (1, 0) for z in range(6, 14) for x in range(2, 6)
]
HEAD_ORDER = [5, 1, 6, 2, 7, 3, 0, 4]
GROUPS = 64
PAIR_ROWS = 8
MASK_OUT = 32768.0
GUIDE_SCALE = 6.0
NORM_EPS = 1e-05
EXPONENT = math.log2(math.e) / math.sqrt(HEAD_DIM)
F32, BF16, I32 = jnp.float32, jnp.bfloat16, jnp.int32
NT = (((1,), (1,)), ((), ()))


def iota(shape, dim):
    return lax.broadcasted_iota(I32, shape, dim)


def ones_where(cond):
    return jnp.where(cond, 1.0, 0.0).astype(BF16)


def one_hot(cond):
    return jnp.where(cond, jnp.ones(cond.shape, BF16), jnp.zeros(cond.shape, BF16))


def matmul(a, b):
    return jnp.dot(a, b, preferred_element_type=F32)


def swap_halves(x):
    return pltpu.roll(x, HEAD_DIM, 1)


def pack_kernel(
    parity_ref,
    qkv_hbm,
    rank_hbm,
    sizes_hbm,
    owner_hbm,
    send_ref,
    row_ref,
    sizes_ref,
    owner_ref,
    rank_ref,
    qkv_ref,
    sem,
):
    sources = (sizes_hbm, owner_hbm, rank_hbm, qkv_hbm)
    targets = (sizes_ref, owner_ref, rank_ref, qkv_ref)
    fetches = [
        pltpu.make_async_copy(src, dst, sem.at[i])
        for i, (src, dst) in enumerate(zip(sources, targets))
    ]
    for fetch in fetches:
        fetch.start()
    heads, tokens = rank_ref.shape
    clusters = sizes_ref.shape[1]
    pairs = heads // 2
    slots = GROUPS * PAIR_ROWS
    before = ones_where(iota((tokens, tokens), 0) < iota((tokens, tokens), 1))
    strict = ones_where(iota((clusters, clusters), 1) < iota((clusters, clusters), 0))
    slots_iota = iota((slots, tokens), 0).astype(jnp.int16)
    for fetch in fetches[:3]:
        fetch.wait()
    sizes = sizes_ref[...]
    low = (sizes & 255).astype(F32).astype(BF16)
    high = (sizes >> 8).astype(F32).astype(BF16)
    starts = lax.dot_general(strict, low, NT, preferred_element_type=F32)
    starts = starts + 256.0 * lax.dot_general(strict, high, NT, preferred_element_type=F32)
    starts = starts.astype(I32).astype(jnp.int16)
    ranks = rank_ref[...].astype(jnp.int16)
    owned = [
        jnp.where(iota((GROUPS, clusters), 0) == owner_ref[h : h + 1, :], 1.0, 0.0)
        for h in range(heads)
    ]
    counts = matmul(jnp.concatenate(owned, axis=0).astype(BF16), before)
    first = iota((GROUPS + 8, clusters), 1) == 0
    dests, labels = [], []
    for h in range(heads):
        nth = jnp.sum(owned[h] * counts[GROUPS * h : GROUPS * (h + 1)], axis=0, keepdims=True)
        label = jnp.where(iota((8, clusters), 0) - 4 * (h % 2) == nth.astype(I32), 1.0, 0.0)
        table = jnp.concatenate([owned[h], label], axis=0)
        step = table - jnp.where(first, 0.0, pltpu.roll(table, 1, 1))
        reached = one_hot(starts[:, h : h + 1] <= ranks[h : h + 1, :])
        rows = matmul(step.astype(BF16), reached)
        dests.append(rows[:GROUPS])
        labels.append(rows[GROUPS:])
    earlier = matmul(jnp.concatenate(dests, axis=0).astype(BF16), before)
    group_id = iota((GROUPS, 1), 0).astype(F32) * float(PAIR_ROWS)
    slot_rows = []
    for h in range(heads):
        offset = group_id
        if h % 2:
            offset = offset + jnp.sum(dests[h - 1], axis=1, keepdims=True)
        ahead = earlier[GROUPS * h : GROUPS * (h + 1)] + offset
        slot = jnp.sum(dests[h] * ahead, axis=0, keepdims=True)
        slot_rows.append(slot)
    slot = jnp.concatenate(slot_rows, axis=0).astype(I32)
    group, place = slot >> 3, slot & 7
    mixed_row = 12 * group + 4 * parity_ref[0] + place
    last_row = 12 * group + 8 - 8 * parity_ref[0] + (place & 3)
    back_row = jnp.where(iota(slot.shape, 0) < 4, mixed_row, last_row)
    row_ref[...] = jnp.concatenate([back_row, place[4:6] >> 2], axis=0).astype(F32)
    left = iota((tokens, 2 * HEAD_DIM), 1) < HEAD_DIM
    lane = iota((tokens, 2 * HEAD_DIM), 1)
    marks = []
    for half in range(2):
        zeros = jnp.zeros((HEAD_DIM, tokens), F32)
        rest = jnp.zeros((HEAD_DIM - 8 * pairs, tokens), F32)
        marks.append(jnp.transpose(jnp.concatenate([zeros, *labels[half::2], rest], axis=0)))
    fetches[3].wait()
    values = []
    for j in range(pairs):
        cols = slice(2 * HEAD_DIM * j, 2 * HEAD_DIM * (j + 1))
        own = (lane >= HEAD_DIM + 8 * j) & (lane < HEAD_DIM + 8 * (j + 1))
        even, odd = (jnp.where(own, m, 0.0) for m in marks)
        q, k, v = (qkv_ref[i, :, cols].astype(F32) for i in range(3))
        qs, ks, vs = swap_halves(q), swap_halves(k), swap_halves(v)
        even = jnp.concatenate([jnp.where(left, q, ks), jnp.where(left, v, even)], axis=1)
        odd = jnp.concatenate([jnp.where(left, qs, k), jnp.where(left, vs, odd)], axis=1)
        place = jnp.concatenate(
            [
                one_hot(slots_iota == slot_rows[h].astype(I32).astype(jnp.int16))
                for h in (2 * j, 2 * j + 1)
            ],
            axis=1,
        )
        sorted_rows = matmul(place, jnp.concatenate([even, odd], axis=0).astype(BF16))
        send_ref[:, 8 * j : 8 * (j + 1), :] = (
            sorted_rows[:, : 2 * HEAD_DIM].reshape(GROUPS, 8, 2 * HEAD_DIM).astype(BF16)
        )
        values.append(sorted_rows[:, 2 * HEAD_DIM :])
    left = iota((slots, 2 * HEAD_DIM), 1) < HEAD_DIM
    first = jnp.where(left, values[0], swap_halves(values[1]))
    second = jnp.where(left, values[2], values[0] + values[1] + values[2])
    send_ref[:, 24:32, :] = first.reshape(GROUPS, 8, 2 * HEAD_DIM).astype(BF16)
    send_ref[:, 32:40, :] = second.reshape(GROUPS, 8, 2 * HEAD_DIM).astype(BF16)


def attend_kernel(recv_ref, back_ref):
    rows = GROUPS * PAIR_ROWS
    wide = 2 * HEAD_DIM

    def block(k):
        return recv_ref[:, 8 * k : 8 * (k + 1), :].reshape(rows, wide)

    lane = iota((rows, wide), 1)
    left = lane < HEAD_DIM
    values_01 = block(3)
    marks = block(4).astype(F32)
    values_2 = jnp.where(left, marks, swap_halves(marks)).astype(BF16)

    def operands(j):
        qk = block(j).astype(F32)
        own = (lane >= HEAD_DIM + 8 * j) & (lane < HEAD_DIM + 8 * (j + 1))
        a = jnp.where(left, qk, marks).astype(BF16)
        b = jnp.where(
            left, swap_halves(qk), jnp.where(own, MASK_OUT * (marks - 1.0), 0.0)
        ).astype(BF16)
        return a, b

    def score(ab):
        return lax.dot_general(ab[0], ab[1], NT, preferred_element_type=F32)

    def softmax(scores):
        largest = jnp.max(scores, axis=1, keepdims=True)
        expo = jnp.exp2((scores - largest) * EXPONENT)
        totals = jnp.sum(expo, axis=1, keepdims=True)
        return (expo * (1.0 / totals)).astype(BF16)

    ab = [operands(j) for j in range(3)]
    scores = [score(x) for x in ab]
    probs = [softmax(x) for x in scores]
    outs = [matmul(p, values_2 if j == 2 else values_01) for j, p in enumerate(probs)]
    shape = (GROUPS // 2, 2, 8, wide)
    mixed = jnp.where(left, outs[0], outs[1]).reshape(shape).astype(BF16)
    back_ref[:, 0:8, :] = mixed[:, 0]
    back_ref[:, 16:24, :] = mixed[:, 1]
    last = outs[2].reshape(GROUPS, 8, wide)
    turned = pltpu.roll(last, 4, 1).reshape(shape)
    last = last.reshape(shape)
    near = iota((GROUPS // 2, 8, wide), 2) < HEAD_DIM
    upper = iota((GROUPS // 2, 8, wide), 1) < 4
    last = jnp.where(
        upper,
        jnp.where(near, last[:, 0], turned[:, 0]),
        jnp.where(near, turned[:, 1], last[:, 1]),
    )
    back_ref[:, 8:16, :] = last.astype(BF16)


def finish_kernel(parity_ref, back_ref, row_ref, un_ref, att_ref, guided_ref):
    tokens = row_ref.shape[1]
    rows = back_ref.shape[0]
    wide = 2 * HEAD_DIM
    table = jnp.transpose(row_ref[...])
    row = table.astype(I32).astype(jnp.int16)
    pos = iota((tokens, rows), 1).astype(jnp.int16)
    kept = back_ref[...]
    quarter = iota((rows // 24, 24, wide), 1) >> 2
    own = quarter == 2 - 2 * parity_ref[0]
    own = (own | (quarter == 5 - 2 * parity_ref[0])).reshape(rows, wide)
    apart = kept.astype(F32)
    apart = jnp.concatenate([jnp.where(own, 0.0, apart), jnp.where(own, apart, 0.0)], axis=1)
    apart = apart.astype(BF16)
    left = iota((tokens, wide), 1) < HEAD_DIM
    hits = [row[:, h : h + 1] == pos for h in range(6)]
    both = [matmul(one_hot(hits[h] | hits[h + 4]), apart) for h in range(2)]
    found = [x[:, :wide] for x in both] + [matmul(one_hot(hits[h]), kept) for h in (2, 3)]
    found += [x[:, wide:] for x in both]
    for j in range(3):
        low, high = found[2 * j], found[2 * j + 1]
        if j == 0:
            high = swap_halves(high)
        elif j == 1:
            low = swap_halves(low)
        else:
            low = jnp.where(table[:, 6:7] > 0.5, swap_halves(low), low)
            high = jnp.where(table[:, 7:8] > 0.5, high, swap_halves(high))
        att = jnp.where(left, low, high)
        cols = slice(wide * j, wide * (j + 1))
        att_ref[:, cols] = att.astype(BF16)
        un = un_ref[:, cols].astype(F32)
        guided = (un + GUIDE_SCALE * (att - un)).astype(BF16)
        parts, count, _ = guided_ref.shape
        for i in range(parts):
            at = HEAD_ORDER[i] * count
            guided_ref[i, :, cols] = guided[at : at + count]


def last_kernel(rows_ref, gain_ref, bias_ref, att_ref, c0_ref, c1_ref, c2_ref, *refs):
    outs, buffers, sem = refs[:5], refs[5:9], refs[9]
    copies = []

    def send(ref, out):
        copies.append(pltpu.make_async_copy(ref, out, sem.at[len(copies)]))
        copies[-1].start()

    send(att_ref, outs[1])
    chunk = att_ref.shape[0] // 4
    for start in range(0, att_ref.shape[0], chunk):
        rows = slice(start, start + chunk)
        first = (att_ref[rows].astype(F32) - c0_ref[rows].astype(F32)) * 0.5
        second = (first - c1_ref[rows].astype(F32)) * 0.5
        third = (second - c2_ref[rows].astype(F32)) * 0.5
        for i, term in enumerate((first, second, third)):
            buffers[1 + i][rows] = term.astype(BF16)
    for i in range(3):
        send(buffers[1 + i], outs[2 + i])
    parts, _, width = rows_ref.shape
    total = parts * width
    blocks = [rows_ref[i].astype(F32) for i in range(parts)]
    mean = sum(jnp.sum(b, axis=1, keepdims=True) for b in blocks) * (1.0 / total)
    blocks = [b - mean for b in blocks]
    var = sum(jnp.sum(b * b, axis=1, keepdims=True) for b in blocks) * (1.0 / total)
    scale = lax.rsqrt(var + NORM_EPS)
    for i, b in enumerate(blocks):
        cols = slice(width * HEAD_ORDER[i], width * (HEAD_ORDER[i] + 1))
        buffers[0][:, cols] = (b * scale * gain_ref[:, cols] + bias_ref[:, cols]).astype(BF16)
    send(buffers[0], outs[0])
    for copy in copies:
        copy.wait()


VMEM = pl.BlockSpec(memory_space=pltpu.VMEM)
HBM = pl.BlockSpec(memory_space=pl.ANY)
SMEM = pl.BlockSpec(memory_space=pltpu.SMEM)


def in_vmem(x):
    return pltpu.with_memory_space_constraint(x, pltpu.VMEM)


def call(kernel, outs, in_specs, *args, **kw):
    return pl.pallas_call(
        kernel, out_shape=outs, in_specs=in_specs, out_specs=[VMEM] * len(outs), **kw
    )(*args)


def pack(parity, qkv, token_rank, cluster_sizes, cluster_owner, **kw):
    tokens = token_rank.shape[1]
    outs = [pltpu.VMEM((GROUPS, 40, 128), BF16), pltpu.VMEM((8, tokens), F32)]
    scratch = [pltpu.VMEM(x.shape, x.dtype) for x in (cluster_sizes, cluster_owner, token_rank, qkv)]
    scratch.append(pltpu.SemaphoreType.DMA((4,)))
    args = (parity, qkv, token_rank, cluster_sizes, cluster_owner)
    specs = [SMEM, HBM, HBM, HBM, HBM]
    return call(pack_kernel, outs, specs, *args, scratch_shapes=scratch, **kw)


def attend(arrived, **kw):
    outs = [pltpu.VMEM((GROUPS // 2, 24, 128), BF16)]
    back = call(attend_kernel, outs, [VMEM], in_vmem(arrived), **kw)[0]
    return back.reshape(GROUPS, 3, 4, 128)


def finish(parity, back, table, un, **kw):
    outs = [pltpu.VMEM(un.shape, BF16), pltpu.VMEM((8, un.shape[0] // 8, un.shape[1]), BF16)]
    args = [in_vmem(x) for x in (back.reshape(GROUPS * 12, 128), table, un)]
    return call(finish_kernel, outs, [SMEM] + [VMEM] * 3, parity, *args, **kw)


def last(rows, gain, bias, att, c0, c1, c2, **kw):
    parts, count, width = rows.shape
    shapes = [(count, parts * width)] + [att.shape] * 4
    args = [in_vmem(x) for x in (rows, gain.reshape(1, -1), bias.reshape(1, -1), att, c0, c1, c2)]
    return pl.pallas_call(
        last_kernel,
        out_shape=[jax.ShapeDtypeStruct(s, BF16) for s in shapes],
        in_specs=[VMEM] * 7,
        out_specs=[HBM] * 5,
        scratch_shapes=[pltpu.VMEM(s, BF16) for s in shapes[:1] + shapes[2:]]
        + [pltpu.SemaphoreType.DMA((5,))],
        **kw,
    )(*args)


def exchange(x, axis, order):
    return lax.all_to_all(x, axis, 0, 0, axis_index_groups=[order], tiled=True)


def on_device(qkv, rank, sizes, owner, c0, c1, c2, un, gain, bias):
    parity = ((lax.axis_index("tok") >> 4) & 1).reshape(1)
    send, table = pack(parity, qkv, rank, sizes, owner)
    arrived = exchange(send, "tok", TOK_ORDER)
    back = exchange(attend(arrived), "tok", TOK_ORDER)
    att, guided = finish(parity, back, table, un)
    rows = exchange(guided, "head", HEAD_ORDER)
    return tuple(last(rows, gain, bias, att, c0, c1, c2))


def solution(mesh):
    cached = P("tok", "head")
    in_specs = (P(None, "tok", "head"), P("head", "tok"), P("head", None), P("head", None))
    in_specs = in_specs + (cached,) * 4 + (P(), P())
    out_specs = (P(("tok", "head"), None),) + (cached,) * 4
    return jax.shard_map(
        on_device, mesh=mesh, in_specs=in_specs, out_specs=out_specs, check_vma=False
    )
```

```python
import math

import jax
import jax.numpy as jnp
from jax import lax
from jax.experimental import pallas as pl
from jax.experimental.pallas import tpu as pltpu
from jax.sharding import PartitionSpec as P

HEAD_DIM = 64
TOK_ORDER = [
    (16 * (x % 4)) + 2 * (z % 8) + core for core in (1, 0) for z in range(6, 14) for x in range(3, 7)
]
HEAD_ORDER = [5, 1, 6, 2, 7, 3, 0, 4]
GROUPS = 64
PAIR_ROWS = 8
MASK_OUT = 32768.0
GUIDE_SCALE = 6.0
NORM_EPS = 1e-05
EXPONENT = math.log2(math.e) / math.sqrt(HEAD_DIM)
F32, BF16, I32 = jnp.float32, jnp.bfloat16, jnp.int32
NT = (((1,), (1,)), ((), ()))


def iota(shape, dim):
    return lax.broadcasted_iota(I32, shape, dim)


def ones_where(cond):
    return jnp.where(cond, 1.0, 0.0).astype(BF16)


def one_hot(cond):
    return jnp.where(cond, jnp.ones(cond.shape, BF16), jnp.zeros(cond.shape, BF16))


def matmul(a, b):
    return jnp.dot(a, b, preferred_element_type=F32)


def swap_halves(x):
    return pltpu.roll(x, HEAD_DIM, 1)


def pack_kernel(
    parity_ref,
    qkv_hbm,
    rank_hbm,
    sizes_hbm,
    owner_hbm,
    send_ref,
    row_ref,
    sizes_ref,
    owner_ref,
    rank_ref,
    qkv_ref,
    sem,
):
    sources = (sizes_hbm, owner_hbm, rank_hbm, qkv_hbm)
    targets = (sizes_ref, owner_ref, rank_ref, qkv_ref)
    fetches = [
        pltpu.make_async_copy(src, dst, sem.at[i])
        for i, (src, dst) in enumerate(zip(sources, targets))
    ]
    for fetch in fetches:
        fetch.start()
    heads, tokens = rank_ref.shape
    clusters = sizes_ref.shape[1]
    pairs = heads // 2
    slots = GROUPS * PAIR_ROWS
    before = ones_where(iota((tokens, tokens), 0) < iota((tokens, tokens), 1))
    strict = ones_where(iota((clusters, clusters), 1) < iota((clusters, clusters), 0))
    slots_iota = iota((slots, tokens), 0).astype(jnp.int16)
    for fetch in fetches[:3]:
        fetch.wait()
    sizes = sizes_ref[...]
    low = (sizes & 255).astype(F32).astype(BF16)
    high = (sizes >> 8).astype(F32).astype(BF16)
    starts = lax.dot_general(strict, low, NT, preferred_element_type=F32)
    starts = starts + 256.0 * lax.dot_general(strict, high, NT, preferred_element_type=F32)
    starts = starts.astype(I32).astype(jnp.int16)
    ranks = rank_ref[...].astype(jnp.int16)
    owned = [
        jnp.where(iota((GROUPS, clusters), 0) == owner_ref[h : h + 1, :], 1.0, 0.0)
        for h in range(heads)
    ]
    counts = matmul(jnp.concatenate(owned, axis=0).astype(BF16), before)
    first = iota((GROUPS + 8, clusters), 1) == 0
    dests, labels = [], []
    for h in range(heads):
        nth = jnp.sum(owned[h] * counts[GROUPS * h : GROUPS * (h + 1)], axis=0, keepdims=True)
        label = jnp.where(iota((8, clusters), 0) - 4 * (h % 2) == nth.astype(I32), 1.0, 0.0)
        table = jnp.concatenate([owned[h], label], axis=0)
        step = table - jnp.where(first, 0.0, pltpu.roll(table, 1, 1))
        reached = one_hot(starts[:, h : h + 1] <= ranks[h : h + 1, :])
        rows = matmul(step.astype(BF16), reached)
        dests.append(rows[:GROUPS])
        labels.append(rows[GROUPS:])
    earlier = matmul(jnp.concatenate(dests, axis=0).astype(BF16), before)
    group_id = iota((GROUPS, 1), 0).astype(F32) * float(PAIR_ROWS)
    slot_rows, places = [], []
    for h in range(heads):
        offset = group_id
        if h % 2:
            offset = offset + jnp.sum(dests[h - 1], axis=1, keepdims=True)
        ahead = earlier[GROUPS * h : GROUPS * (h + 1)] + offset
        slot = jnp.sum(dests[h] * ahead, axis=0, keepdims=True)
        slot_rows.append(slot)
        places.append(one_hot(slots_iota == slot.astype(I32).astype(jnp.int16)))
    slot = jnp.concatenate(slot_rows, axis=0).astype(I32)
    group, place = slot >> 3, slot & 7
    mixed_row = 12 * group + 4 * parity_ref[0] + place
    last_row = 12 * group + 8 - 8 * parity_ref[0] + (place & 3)
    back_row = jnp.where(iota(slot.shape, 0) < 4, mixed_row, last_row)
    row_ref[...] = jnp.concatenate([back_row, place[4:6] >> 2], axis=0).astype(F32)
    left = iota((tokens, 2 * HEAD_DIM), 1) < HEAD_DIM
    lane = iota((tokens, 2 * HEAD_DIM), 1)
    marks = []
    for half in range(2):
        zeros = jnp.zeros((HEAD_DIM, tokens), F32)
        rest = jnp.zeros((HEAD_DIM - 8 * pairs, tokens), F32)
        marks.append(jnp.transpose(jnp.concatenate([zeros, *labels[half::2], rest], axis=0)))
    fetches[3].wait()
    values = []
    for j in range(pairs):
        cols = slice(2 * HEAD_DIM * j, 2 * HEAD_DIM * (j + 1))
        own = (lane >= HEAD_DIM + 8 * j) & (lane < HEAD_DIM + 8 * (j + 1))
        even, odd = (jnp.where(own, m, 0.0) for m in marks)
        q, k, v = (qkv_ref[i, :, cols].astype(F32) for i in range(3))
        qs, ks, vs = swap_halves(q), swap_halves(k), swap_halves(v)
        even = jnp.concatenate([jnp.where(left, q, ks), jnp.where(left, v, even)], axis=1)
        odd = jnp.concatenate([jnp.where(left, qs, k), jnp.where(left, vs, odd)], axis=1)
        place = jnp.concatenate(places[2 * j : 2 * j + 2], axis=1)
        sorted_rows = matmul(place, jnp.concatenate([even, odd], axis=0).astype(BF16))
        send_ref[:, 8 * j : 8 * (j + 1), :] = (
            sorted_rows[:, : 2 * HEAD_DIM].reshape(GROUPS, 8, 2 * HEAD_DIM).astype(BF16)
        )
        values.append(sorted_rows[:, 2 * HEAD_DIM :])
    left = iota((slots, 2 * HEAD_DIM), 1) < HEAD_DIM
    first = jnp.where(left, values[0], swap_halves(values[1]))
    second = jnp.where(left, values[2], values[0] + values[1] + values[2])
    send_ref[:, 24:32, :] = first.reshape(GROUPS, 8, 2 * HEAD_DIM).astype(BF16)
    send_ref[:, 32:40, :] = second.reshape(GROUPS, 8, 2 * HEAD_DIM).astype(BF16)


def attend_kernel(recv_ref, back_ref):
    rows = GROUPS * PAIR_ROWS
    wide = 2 * HEAD_DIM

    def block(k):
        return recv_ref[:, 8 * k : 8 * (k + 1), :].reshape(rows, wide)

    lane = iota((rows, wide), 1)
    left = lane < HEAD_DIM
    values_01 = block(3)
    marks = block(4).astype(F32)
    values_2 = jnp.where(left, marks, swap_halves(marks)).astype(BF16)

    def operands(j):
        qk = block(j).astype(F32)
        own = (lane >= HEAD_DIM + 8 * j) & (lane < HEAD_DIM + 8 * (j + 1))
        a = jnp.where(left, qk, marks).astype(BF16)
        b = jnp.where(
            left, swap_halves(qk), jnp.where(own, MASK_OUT * (marks - 1.0), 0.0)
        ).astype(BF16)
        return a, b

    def score(ab):
        return lax.dot_general(ab[0], ab[1], NT, preferred_element_type=F32)

    def softmax(scores):
        largest = jnp.max(scores, axis=1, keepdims=True)
        expo = jnp.exp2((scores - largest) * EXPONENT)
        totals = jnp.sum(expo, axis=1, keepdims=True)
        return (expo * (1.0 / totals)).astype(BF16)

    ab = [operands(j) for j in range(3)]
    scores = [score(x) for x in ab]
    probs = [softmax(x) for x in scores]
    outs = [matmul(p, values_2 if j == 2 else values_01) for j, p in enumerate(probs)]
    shape = (GROUPS // 2, 2, 8, wide)
    mixed = jnp.where(left, outs[0], outs[1]).reshape(shape).astype(BF16)
    back_ref[:, 0:8, :] = mixed[:, 0]
    back_ref[:, 16:24, :] = mixed[:, 1]
    last = outs[2].reshape(GROUPS, 8, wide)
    turned = pltpu.roll(last, 4, 1).reshape(shape)
    last = last.reshape(shape)
    near = iota((GROUPS // 2, 8, wide), 2) < HEAD_DIM
    upper = iota((GROUPS // 2, 8, wide), 1) < 4
    last = jnp.where(
        upper,
        jnp.where(near, last[:, 0], turned[:, 0]),
        jnp.where(near, turned[:, 1], last[:, 1]),
    )
    back_ref[:, 8:16, :] = last.astype(BF16)


def finish_kernel(parity_ref, back_ref, row_ref, un_ref, att_ref, guided_ref):
    tokens = row_ref.shape[1]
    rows = back_ref.shape[0]
    wide = 2 * HEAD_DIM
    table = jnp.transpose(row_ref[...])
    row = table.astype(I32).astype(jnp.int16)
    pos = iota((tokens, rows), 1).astype(jnp.int16)
    kept = back_ref[...]
    quarter = iota((rows // 24, 24, wide), 1) >> 2
    own = quarter == 2 - 2 * parity_ref[0]
    own = (own | (quarter == 5 - 2 * parity_ref[0])).reshape(rows, wide)
    apart = kept.astype(F32)
    apart = jnp.concatenate([jnp.where(own, 0.0, apart), jnp.where(own, apart, 0.0)], axis=1)
    apart = apart.astype(BF16)
    left = iota((tokens, wide), 1) < HEAD_DIM
    hits = [row[:, h : h + 1] == pos for h in range(6)]
    both = [matmul(one_hot(hits[h] | hits[h + 4]), apart) for h in range(2)]
    found = [x[:, :wide] for x in both] + [matmul(one_hot(hits[h]), kept) for h in (2, 3)]
    found += [x[:, wide:] for x in both]
    for j in range(3):
        low, high = found[2 * j], found[2 * j + 1]
        if j == 0:
            high = swap_halves(high)
        elif j == 1:
            low = swap_halves(low)
        else:
            low = jnp.where(table[:, 6:7] > 0.5, swap_halves(low), low)
            high = jnp.where(table[:, 7:8] > 0.5, high, swap_halves(high))
        att = jnp.where(left, low, high)
        cols = slice(wide * j, wide * (j + 1))
        att_ref[:, cols] = att.astype(BF16)
        un = un_ref[:, cols].astype(F32)
        guided = (un + GUIDE_SCALE * (att - un)).astype(BF16)
        parts, count, _ = guided_ref.shape
        for i in range(parts):
            at = HEAD_ORDER[i] * count
            guided_ref[i, :, cols] = guided[at : at + count]


def last_kernel(rows_ref, gain_ref, bias_ref, att_ref, c0_ref, c1_ref, c2_ref, *refs):
    outs, buffers, sem = refs[:5], refs[5:9], refs[9]
    copies = []

    def send(ref, out):
        copies.append(pltpu.make_async_copy(ref, out, sem.at[len(copies)]))
        copies[-1].start()

    send(att_ref, outs[1])
    chunk = att_ref.shape[0] // 4
    for start in range(0, att_ref.shape[0], chunk):
        rows = slice(start, start + chunk)
        first = (att_ref[rows].astype(F32) - c0_ref[rows].astype(F32)) * 0.5
        second = (first - c1_ref[rows].astype(F32)) * 0.5
        third = (second - c2_ref[rows].astype(F32)) * 0.5
        for i, term in enumerate((first, second, third)):
            buffers[1 + i][rows] = term.astype(BF16)
    for i in range(3):
        send(buffers[1 + i], outs[2 + i])
    parts, _, width = rows_ref.shape
    total = parts * width
    blocks = [rows_ref[i].astype(F32) for i in range(parts)]
    mean = sum(jnp.sum(b, axis=1, keepdims=True) for b in blocks) * (1.0 / total)
    blocks = [b - mean for b in blocks]
    var = sum(jnp.sum(b * b, axis=1, keepdims=True) for b in blocks) * (1.0 / total)
    scale = lax.rsqrt(var + NORM_EPS)
    for i, b in enumerate(blocks):
        cols = slice(width * HEAD_ORDER[i], width * (HEAD_ORDER[i] + 1))
        buffers[0][:, cols] = (b * scale * gain_ref[:, cols] + bias_ref[:, cols]).astype(BF16)
    send(buffers[0], outs[0])
    for copy in copies:
        copy.wait()


VMEM = pl.BlockSpec(memory_space=pltpu.VMEM)
HBM = pl.BlockSpec(memory_space=pl.ANY)
SMEM = pl.BlockSpec(memory_space=pltpu.SMEM)


def in_vmem(x):
    return pltpu.with_memory_space_constraint(x, pltpu.VMEM)


def call(kernel, outs, in_specs, *args, **kw):
    return pl.pallas_call(
        kernel, out_shape=outs, in_specs=in_specs, out_specs=[VMEM] * len(outs), **kw
    )(*args)


def pack(parity, qkv, token_rank, cluster_sizes, cluster_owner, **kw):
    tokens = token_rank.shape[1]
    outs = [pltpu.VMEM((GROUPS, 40, 128), BF16), pltpu.VMEM((8, tokens), F32)]
    scratch = [pltpu.VMEM(x.shape, x.dtype) for x in (cluster_sizes, cluster_owner, token_rank, qkv)]
    scratch.append(pltpu.SemaphoreType.DMA((4,)))
    args = (parity, qkv, token_rank, cluster_sizes, cluster_owner)
    specs = [SMEM, HBM, HBM, HBM, HBM]
    return call(pack_kernel, outs, specs, *args, scratch_shapes=scratch, **kw)


def attend(arrived, **kw):
    outs = [pltpu.VMEM((GROUPS // 2, 24, 128), BF16)]
    back = call(attend_kernel, outs, [VMEM], in_vmem(arrived), **kw)[0]
    return back.reshape(GROUPS, 3, 4, 128)


def finish(parity, back, table, un, **kw):
    outs = [pltpu.VMEM(un.shape, BF16), pltpu.VMEM((8, un.shape[0] // 8, un.shape[1]), BF16)]
    args = [in_vmem(x) for x in (back.reshape(GROUPS * 12, 128), table, un)]
    return call(finish_kernel, outs, [SMEM] + [VMEM] * 3, parity, *args, **kw)


def last(rows, gain, bias, att, c0, c1, c2, **kw):
    parts, count, width = rows.shape
    shapes = [(count, parts * width)] + [att.shape] * 4
    args = [in_vmem(x) for x in (rows, gain.reshape(1, -1), bias.reshape(1, -1), att, c0, c1, c2)]
    return pl.pallas_call(
        last_kernel,
        out_shape=[jax.ShapeDtypeStruct(s, BF16) for s in shapes],
        in_specs=[VMEM] * 7,
        out_specs=[HBM] * 5,
        scratch_shapes=[pltpu.VMEM(s, BF16) for s in shapes[:1] + shapes[2:]]
        + [pltpu.SemaphoreType.DMA((5,))],
        **kw,
    )(*args)


def exchange(x, axis, order):
    return lax.all_to_all(x, axis, 0, 0, axis_index_groups=[order], tiled=True)


def on_device(qkv, rank, sizes, owner, c0, c1, c2, un, gain, bias):
    parity = (((lax.axis_index("tok") >> 4) + 1) & 1).reshape(1)
    send, table = pack(parity, qkv, rank, sizes, owner)
    arrived = exchange(send, "tok", TOK_ORDER)
    back = exchange(attend(arrived), "tok", TOK_ORDER)
    att, guided = finish(parity, back, table, un)
    rows = exchange(guided, "head", HEAD_ORDER)
    return tuple(last(rows, gain, bias, att, c0, c1, c2))


def solution(mesh):
    cached = P("tok", "head")
    in_specs = (P(None, "tok", "head"), P("head", "tok"), P("head", None), P("head", None))
    in_specs = in_specs + (cached,) * 4 + (P(), P())
    out_specs = (P(("tok", "head"), None),) + (cached,) * 4
    return jax.shard_map(
        on_device, mesh=mesh, in_specs=in_specs, out_specs=out_specs, check_vma=False
    )
```
